768 devices in a mesh: node: 48 (over x_hi, z, core), rep: 16 (over y, x_lo).
Axes of the slice: x: 4 (x_hi: 2, x_lo: 2; x = x_hi * 2 + x_lo), y: 8, z: 12, core: 2. Of those that a mesh axis runs over, the one named last changes fastest.
Arguments:
- aggregated: bfloat16 [196608, 512], P(('node', 'rep')), may hold values from -6 to 6
- cotangent: bfloat16 [196608, 512], P(('node', 'rep')), may hold values from -6 to 6
- kernel_in: bfloat16 [512, 2048], P(None, 'rep'), may hold values from -0.25 to 0.25
- kernel_out: bfloat16 [2048, 512], P('rep'), may hold values from -0.125 to 0.125
- tile_values: bfloat16 [768, 4, 256, 256], P(('node', 'rep')), may hold values from -0.5 to 0.5
- tile_cols: int32 [768, 4], P(('node', 'rep')), may hold values from 0 to 2, as said below
- tile_count: int32 [768], P(('node', 'rep')), may hold values from 1 to 4, as said below
Outputs:
- grad_nodes: bfloat16 [196608, 512], P(('node', 'rep'))
- grad_in: float32 [512, 2048], P(None, 'rep')
- grad_out: float32 [2048, 512], P('rep')
The draws below stay inside these ranges and needn't reach their ends.
Inputs may be any that keep to these rules, and one draw needn't show every extreme that they name: tile_cols 0, 1 and 2 name the block of the previous cycle position with the same rep index, the block itself and that of the next cycle position; slots at or past tile_count are ignored. `tile_count`: some block row has all 4 slots live.
All inputs are finite; a program needn't handle non-finite values.
Results may differ from the reference program's by a relative error of at most 0.024.
Values may be sent and summed in bfloat16 or wider, within the bound.
A program may use at most 64 MiB of HBM per device.

```python
import math
import jax
import jax.numpy as jnp

D = 512
H = 2048
ROW_DEV = 256
MAXT = 4
NBLK = 768
NODES = 196608
N_REP = 16


def draw_tile_count(key, part):
    counts = jax.random.randint(key, (NBLK,), 1, MAXT + 1).astype(jnp.int32)
    return counts.at[0].set(MAXT)


def draw_tile_cols(key, part):
    columns = jax.random.randint(key, (NBLK, MAXT), 0, 3).astype(jnp.int32)
    return columns.at[0, 0].set(0).at[0, 1].set(2)


def shard_levels(own_key, dims, pieces, smallest, largest):
    def one(axis_at, parts):
        steps = jax.random.uniform(jax.random.fold_in(jax.random.fold_in(own_key, 6), axis_at), (parts,), jnp.float32, smallest / len(pieces), largest / len(pieces))
        return jnp.repeat(jnp.exp(steps), dims[axis_at] // parts).reshape((-1,) + (1,) * (len(dims) - axis_at - 1))

    gain = one(*pieces[0])
    for cut in pieces[1:]:
        gain = gain * one(*cut)
    return gain


def normal_values(own_key, dims, spread, most, cuts=(), held_as=jnp.bfloat16):
    values = jax.random.normal(own_key, dims, jnp.float32) * spread
    if len(cuts) > 0:
        values = shard_levels(own_key, dims, cuts, -0.22, 0.18) * values
    return jnp.clip(values, min=-most, max=most).astype(held_as)


def setup_inputs(seed: int = 0) -> dict:
    streams_of = jax.random.split(jax.random.key(seed), 8)
    return {
        "aggregated": normal_values(streams_of[0], (NODES, D), 1.0, 6.0, ((0, 768),)),
        "cotangent": normal_values(streams_of[1], (NODES, D), 1.0, 6.0, ((0, 768),)),
        "kernel_in": normal_values(streams_of[2], (D, H), D ** -0.5, 0.25, ((1, 16),)),
        "kernel_out": normal_values(streams_of[3], (H, D), H ** -0.5, 0.125, ((0, 16),)),
        "tile_values": normal_values(streams_of[4], (NBLK, MAXT, ROW_DEV, ROW_DEV), 0.09, 0.5, ((0, 768),)),
        "tile_cols": draw_tile_cols(jax.random.fold_in(streams_of[7], 71), 0),
        "tile_count": draw_tile_count(jax.random.fold_in(streams_of[7], 71), 0),
    }


def gelu_value(pre_act):
    inner = math.sqrt(2.0 / math.pi) * (pre_act + 0.044715 * pre_act * pre_act * pre_act)
    return 0.5 * pre_act * (1.0 + jnp.tanh(inner))

def gelu_slope(pre_act):
    inner = math.sqrt(2.0 / math.pi) * (pre_act + 0.044715 * pre_act * pre_act * pre_act)
    tanh_val = jnp.tanh(inner)
    return 0.5 * (1.0 + tanh_val) + 0.5 * pre_act * (1.0 - tanh_val * tanh_val) * math.sqrt(2.0 / math.pi) * (1.0 + 3.0 * 0.044715 * pre_act * pre_act)

def reference(aggregated, cotangent, kernel_in, kernel_out, tile_values, tile_cols, tile_count):
    norm_factor = 1.0 / math.sqrt(NODES)
    pre_act = jnp.dot(aggregated, kernel_in, preferred_element_type=jnp.float32)
    act_out = gelu_value(pre_act).astype(jnp.bfloat16)
    grad_act = jnp.dot(cotangent, kernel_out.T, preferred_element_type=jnp.float32)
    grad_pre = (grad_act * gelu_slope(pre_act)).astype(jnp.bfloat16)
    grad_out = jnp.dot(act_out.T, cotangent, preferred_element_type=jnp.float32) * norm_factor
    grad_in = jnp.dot(aggregated.T, grad_pre, preferred_element_type=jnp.float32) * norm_factor
    group_width = H // N_REP
    agg_sum = jnp.zeros((NODES, D), jnp.float32)
    for group in range(N_REP):
        lo_col = group * group_width
        piece = jnp.dot(grad_pre[:, lo_col:lo_col + group_width], kernel_in[:, lo_col:lo_col + group_width].T, preferred_element_type=jnp.float32)
        agg_sum = agg_sum + piece.astype(jnp.bfloat16).astype(jnp.float32)
    grad_agg = agg_sum.astype(jnp.bfloat16)
    agg_blocks = grad_agg.reshape(NBLK, ROW_DEV, D).astype(jnp.float32)
    block_ids = jnp.arange(NBLK, dtype=jnp.int32)
    result = cotangent.astype(jnp.float32).reshape(NBLK, ROW_DEV, D)
    for slot_num in range(MAXT):
        tiles = tile_values[:, slot_num].astype(jnp.float32)
        terms = jnp.einsum('brc,brd->bcd', tiles, agg_blocks)
        live = (slot_num < tile_count).astype(jnp.float32)
        terms = terms * live[:, None, None]
        target = ((block_ids + (tile_cols[:, slot_num] - 1) * N_REP) % NBLK).astype(jnp.int32)
        result = result.at[target].add(terms)
    grad_nodes = result.reshape(NODES, D).astype(jnp.bfloat16)
    return (grad_nodes, grad_in, grad_out)
```

```python
import functools
import math

import jax
import jax.numpy as jnp
from jax import lax
from jax.experimental import pallas as pl
from jax.experimental.pallas import tpu as pltpu
from jax.sharding import PartitionSpec as P

MESH = pl.DeviceIdType.MESH
BF16 = jnp.bfloat16
F32 = jnp.float32
X_HI, X_LO, CORES, Z_LO = 2, 2, 2, 3
GELU_C = math.sqrt(2.0 / math.pi)


def dot(left, right):
    return jnp.dot(left, right, preferred_element_type=F32)


def dot_last(left, right):
    return lax.dot_general(left, right, (((1,), (1,)), ((), ())), preferred_element_type=F32)


def mirror(i, ny):
    if i == 0 or i == ny - 1:
        return i
    return i + 1 if i % 2 == 1 else i - 1


def kernel(
    dims,
    agg_ref, cot_ref, kin_ref, kout_ref, tiles_ref, cols_ref, count_ref,
    nodes_ref, grads_ref,
    rows_a, rows_c, at, ct, tiles_t, wts, part, from_core, chain, chain_out, acc, back_out, back_in,
    halo_out, halo_in, pieces, piece_in, triple, triple_in, total,
    s_ring, r_ring, s_core, r_core, s_x, r_x, s_part, r_part, s_chain, r_chain, s_back, r_back,
    s_halo, r_halo, s_piece, r_piece, s_tri, r_tri, s_tot, r_tot, s_swap, r_swap,
):
    ny, nz = dims
    zq_n = nz // Z_LO
    npiece = X_HI * zq_n
    nrow, feat = agg_ref.shape
    node, rep = lax.axis_index("node"), lax.axis_index("rep")
    core = lax.rem(node, CORES)
    z = lax.rem(lax.div(node, CORES), nz)
    xh = lax.div(node, CORES * nz)
    y, xl = lax.div(rep, X_LO), lax.rem(rep, X_LO)
    zq, zr = lax.div(z, Z_LO), lax.rem(z, Z_LO)
    other = 1 - core
    sign = 1 - 2 * core
    nodes = X_HI * nz * CORES

    def dev(xh, xl, y, z, core):
        return (xh * (nz * CORES) + z * CORES + core, y * X_LO + xl)

    mate = dev(xh, xl, y, z, other)
    across = dev(lax.rem(xh + core, X_HI), 1 - xl, y, z, core)
    y_fwd = dev(xh, xl, lax.rem(y + sign + ny, ny), z, core)
    y_bwd = dev(xh, xl, lax.rem(y - sign + ny, ny), z, core)
    nxt = (lax.rem(node + 1, nodes), rep)
    prv = (lax.rem(node + nodes - 1, nodes), rep)
    my_piece = xh * zq_n + zq
    scatter_peers = []
    for j in range(1, npiece):
        pxh = lax.rem(xh + j // zq_n, X_HI)
        pzq = lax.rem(zq + j % zq_n, zq_n)
        scatter_peers.append((j, dev(pxh, xl, y, pzq * Z_LO + zr, core), pxh * zq_n + pzq))
    tri_peers = []
    for j in range(1, Z_LO):
        tri_peers.append((j, dev(xh, xl, y, zq * Z_LO + lax.rem(zr + j, Z_LO), core)))

    barrier = pltpu.get_barrier_semaphore()
    peers = [mate, across, y_fwd, y_bwd, nxt, prv]
    peers += [d for _, d, _ in scatter_peers] + [d for _, d in tri_peers]
    for peer in peers:
        pl.semaphore_signal(barrier, inc=1, device_id=peer, device_id_type=MESH)

    own, far = pl.ds(0, nrow), pl.ds(nrow, nrow)
    wts[0, 0] = kin_ref[...]
    wts[1, 0] = kout_ref[...].T
    rows_a[own] = agg_ref[...]
    rows_c[own] = cot_ref[...]
    at[:, own] = agg_ref[...].T
    ct[:, own] = cot_ref[...].T
    for t in range(tiles_ref.shape[1]):
        tiles_t[t] = tiles_ref[0, t].T
    acc[...] = jnp.zeros_like(acc)
    pl.semaphore_wait(barrier, len(peers))

    started = []

    def send(src, dst, s_sem, r_sem, device):
        copy = pltpu.make_async_remote_copy(
            src_ref=src, dst_ref=dst, send_sem=s_sem, recv_sem=r_sem, device_id=device, device_id_type=MESH
        )
        copy.start()
        started.append(copy)

    def arrive(dst, s_sem, r_sem, device):
        pltpu.make_async_remote_copy(
            src_ref=dst, dst_ref=dst, send_sem=s_sem, recv_sem=r_sem, device_id=device, device_id_type=MESH
        ).wait_recv()

    send(wts.at[core, 0], wts.at[core, 1], s_ring.at[1], r_ring.at[1], y_fwd)
    send(wts.at[core, 0], wts.at[core, 2], s_ring.at[2], r_ring.at[2], y_bwd)
    send(agg_ref, rows_a.at[far], s_x.at[0], r_x.at[0], across)
    send(cot_ref, rows_c.at[far], s_x.at[1], r_x.at[1], across)

    def ring_step(i):
        arrive(wts.at[core, i], s_ring.at[i], r_ring.at[i], y_bwd if i % 2 == 1 else y_fwd)
        if i + 2 < ny:
            send(
                wts.at[core, i], wts.at[core, i + 2], s_ring.at[i + 2], r_ring.at[i + 2],
                y_fwd if i % 2 == 1 else y_bwd,
            )
        j = mirror(i, ny)
        send(wts.at[core, i], wts.at[core, j], s_core.at[i], r_core.at[j], mate)

    def process(i):
        if i > 0:
            arrive(wts.at[other, i], s_core.at[i], r_core.at[i], mate)
        pre = dot(rows_a[...], wts[0, i])
        g_act = dot(rows_c[...], wts[1, i])
        sq = pre * pre
        th = jnp.tanh(GELU_C * (pre + 0.044715 * sq * pre))
        half = 0.5 * (1.0 + th)
        act = (pre * half).astype(BF16)
        slope = half + 0.5 * pre * (1.0 - th * th) * GELU_C * (1.0 + 3.0 * 0.044715 * sq)
        g_pre = (g_act * slope).astype(BF16)
        part[1, i] = dot(ct[...], act).astype(BF16)
        part[0, i] = dot(at[...], g_pre).astype(BF16)
        send(part.at[other, i], from_core.at[mirror(i, ny)], s_part.at[i], r_part.at[mirror(i, ny)], mate)
        acc[...] += dot_last(g_pre, wts[0, i])

    def far_rows():
        arrive(rows_a.at[far], s_x.at[0], r_x.at[0], across)
        arrive(rows_c.at[far], s_x.at[1], r_x.at[1], across)
        at[:, far] = rows_a[far].T
        ct[:, far] = rows_c[far].T

    todo = 0
    for i in range(1, ny):
        ring_step(i)
        if i == 2:
            far_rows()
            process(0)
            todo = 1
        elif i >= 4 and i % 2 == 0:
            process(todo)
            process(todo + 1)
            todo += 2
    for i in range(todo, ny):
        process(i)

    back_out[...] = acc[far].astype(BF16)
    send(back_out, back_in, s_back, r_back, across)

    def chain_step(i):
        arrive(from_core.at[i], s_part.at[i], r_part.at[i], mate)
        tot = part[core, i].astype(F32) + from_core[i].astype(F32)
        if i == 0:
            feeds = [1, 2]
        else:
            feeds = [i + 2] if i + 2 < ny else []
        for f in feeds:
            arrive(chain.at[f], s_chain.at[f], r_chain.at[f], y_fwd if f % 2 == 1 else y_bwd)
            tot = tot + chain[f].astype(F32)
        if i == 0:
            return tot
        chain_out[i] = tot.astype(BF16)
        send(chain_out.at[i], chain.at[i], s_chain.at[i], r_chain.at[i], y_bwd if i % 2 == 1 else y_fwd)

    chain_step(ny - 1)
    chain_step(ny - 2)

    arrive(back_in, s_back, r_back, across)
    g_agg = (acc[own] + back_in[...].astype(F32)).astype(BF16)
    live_count = count_ref[0]
    sums = [None, None, None]
    for t in range(tiles_ref.shape[1]):
        term = dot(tiles_t[t], g_agg)
        for k in range(3):
            on = jnp.logical_and(cols_ref[0, t] == k, t < live_count)
            add = term * jnp.where(on, 1.0, 0.0).astype(F32)
            sums[k] = add if sums[k] is None else sums[k] + add
    halo_out[0] = sums[0].astype(BF16)
    halo_out[1] = sums[2].astype(BF16)
    acc[own] = sums[1] + cot_ref[...].astype(F32)
    send(halo_out.at[0], halo_in.at[0], s_halo.at[0], r_halo.at[0], prv)
    send(halo_out.at[1], halo_in.at[1], s_halo.at[1], r_halo.at[1], nxt)

    for i in range(ny - 3, 0, -1):
        chain_step(i)
    mine = chain_step(0)

    prow = feat // npiece
    for p in range(npiece):
        pieces[p] = mine[p * prow : (p + 1) * prow].astype(BF16)
    for j, peer, p in scatter_peers:
        send(pieces.at[p], piece_in.at[j], s_piece.at[j], r_piece.at[j], peer)

    arrive(halo_in.at[0], s_halo.at[0], r_halo.at[0], nxt)
    arrive(halo_in.at[1], s_halo.at[1], r_halo.at[1], prv)
    nodes_ref[...] = (acc[own] + halo_in[1].astype(F32) + halo_in[0].astype(F32)).astype(BF16)

    tot = pieces[my_piece].astype(F32)
    for j, peer, _ in scatter_peers:
        arrive(piece_in.at[j], s_piece.at[j], r_piece.at[j], peer)
        tot = tot + piece_in[j].astype(F32)
    triple[...] = tot.astype(BF16)
    for j, peer in tri_peers:
        send(triple, triple_in.at[zr], s_tri.at[j], r_tri.at[j], peer)
    triple_in[zr] = triple[...]
    for j, peer in tri_peers:
        arrive(triple_in.at[lax.rem(zr + Z_LO - j, Z_LO)], s_tri.at[j], r_tri.at[j], peer)
    tot = triple_in[0].astype(F32)
    for k in range(1, Z_LO):
        tot = tot + triple_in[k].astype(F32)
    total[core, my_piece] = tot.astype(BF16)
    for j, peer, _ in scatter_peers:
        send(total.at[core, my_piece], total.at[core, my_piece], s_tot.at[j], r_tot.at[j], peer)
    for j, peer, _ in scatter_peers:
        fxh = lax.rem(xh + X_HI - j // zq_n, X_HI)
        fzq = lax.rem(zq + zq_n - j % zq_n, zq_n)
        arrive(total.at[core, fxh * zq_n + fzq], s_tot.at[j], r_tot.at[j], peer)
    send(total.at[core], total.at[core], s_swap, r_swap, mate)
    arrive(total.at[other], s_swap, r_swap, mate)
    for m in range(2):
        for p in range(npiece):
            grads_ref[m, p * prow : (p + 1) * prow, :] = total[m, p]
    for copy in started:
        copy.wait_send()


def local(nz, aggregated, cotangent, kernel_in, kernel_out, tile_values, tile_cols, tile_count):
    nrow, feat = aggregated.shape
    ny = lax.axis_size("rep") // X_LO
    hid = kernel_in.shape[1]
    slots = tile_values.shape[1]
    npiece = X_HI * (nz // Z_LO)
    norm_factor = 1.0 / math.sqrt(nrow * lax.axis_size("node") * lax.axis_size("rep"))
    vmem = lambda shape, dtype=BF16: pltpu.VMEM(shape, dtype)
    dma = lambda *shape: pltpu.SemaphoreType.DMA(shape)
    full = pl.BlockSpec(memory_space=pltpu.VMEM)
    scalars = pl.BlockSpec(memory_space=pltpu.SMEM)
    grad_nodes, grads = pl.pallas_call(
        functools.partial(kernel, (ny, nz)),
        out_shape=(
            jax.ShapeDtypeStruct((nrow, feat), BF16),
            jax.ShapeDtypeStruct((2, feat, hid), BF16),
        ),
        in_specs=[full] * 5 + [scalars] * 2,
        out_specs=(full, full),
        scratch_shapes=[
            vmem((2 * nrow, feat)),
            vmem((2 * nrow, feat)),
            vmem((feat, 2 * nrow)),
            vmem((feat, 2 * nrow)),
            vmem((slots, nrow, nrow)),
            vmem((2, ny, feat, hid)),
            vmem((2, ny, feat, hid)),
            vmem((ny, feat, hid)),
            vmem((ny, feat, hid)),
            vmem((ny, feat, hid)),
            vmem((2 * nrow, feat), F32),
            vmem((nrow, feat)),
            vmem((nrow, feat)),
            vmem((2, nrow, feat)),
            vmem((2, nrow, feat)),
            vmem((npiece, feat // npiece, hid)),
            vmem((npiece, feat // npiece, hid)),
            vmem((feat // npiece, hid)),
            vmem((Z_LO, feat // npiece, hid)),
            vmem((2, npiece, feat // npiece, hid)),
            dma(ny), dma(ny),
            dma(ny), dma(ny),
            dma(2), dma(2),
            dma(ny), dma(ny),
            dma(ny), dma(ny),
            pltpu.SemaphoreType.DMA, pltpu.SemaphoreType.DMA,
            dma(2), dma(2),
            dma(npiece), dma(npiece),
            dma(Z_LO), dma(Z_LO),
            dma(npiece), dma(npiece),
            pltpu.SemaphoreType.DMA, pltpu.SemaphoreType.DMA,
        ],
        compiler_params=pltpu.CompilerParams(
            collective_id=0, has_side_effects=True, vmem_limit_bytes=48 << 20
        ),
    )(aggregated, cotangent, kernel_in, kernel_out, tile_values, tile_cols, tile_count)
    grad_in = grads[0].astype(F32) * norm_factor
    grad_out = grads[1].T.astype(F32) * norm_factor
    return (grad_nodes, grad_in, grad_out)


def solution(mesh):
    nz = mesh.shape["node"] // (X_HI * CORES)
    return jax.shard_map(
        functools.partial(local, nz),
        mesh=mesh,
        in_specs=(
            P(("node", "rep"), None),
            P(("node", "rep"), None),
            P(None, "rep"),
            P("rep", None),
            P(("node", "rep"), None, None, None),
            P(("node", "rep"), None),
            P(("node", "rep")),
        ),
        out_specs=(P(("node", "rep"), None), P(None, "rep"), P("rep", None)),
        check_vma=False,
    )
```

```python
import functools
import math

import jax
import jax.numpy as jnp
from jax import lax
from jax.experimental import pallas as pl
from jax.experimental.pallas import tpu as pltpu
from jax.sharding import PartitionSpec as P

MESH = pl.DeviceIdType.MESH
BF16 = jnp.bfloat16
F32 = jnp.float32
X_HI, X_LO, CORES, NY, Z_IN = 2, 2, 2, 8, 4
HALF = NY // 2
GELU_C = math.sqrt(2.0 / math.pi)
N_SEM = 64


def dot(left, right):
    return jnp.dot(left, right, preferred_element_type=F32)


def dot_last(left, right):
    return lax.dot_general(left, right, (((1,), (1,)), ((), ())), preferred_element_type=F32)


def gelu_pair(pre, g_act):
    sq = pre * pre
    th = jnp.tanh(GELU_C * (pre + 0.044715 * sq * pre))
    half = 0.5 * (1.0 + th)
    slope = half + 0.5 * pre * (1.0 - th * th) * GELU_C * (1.0 + 3.0 * 0.044715 * sq)
    return (pre * half).astype(BF16), (g_act * slope).astype(BF16)


def kernel(
    nz,
    agg_ref, cot_ref, kin_ref, kout_ref, tiles_ref, cols_ref, count_ref,
    nodes_ref, gin_ref, gout_ref,
    rows_a, rows_c, at, ct, tiles, w_in, w_out, act, gpre, part, first, first_out, mid_in, fin_in,
    acc, back_out, back_in, halo_out, halo_in, pieces, piece_in, triple, triple_in, total,
    s_sem, r_sem, l_sem,
):
    zg_n = nz // Z_IN
    npiece = X_HI * Z_IN
    nrow, feat = agg_ref.shape
    node, rep = lax.axis_index("node"), lax.axis_index("rep")
    core = lax.rem(node, CORES)
    z = lax.rem(lax.div(node, CORES), nz)
    xh = lax.div(node, CORES * nz)
    y, xl = lax.div(rep, X_LO), lax.rem(rep, X_LO)
    zg, zi = lax.div(z, Z_IN), lax.rem(z, Z_IN)
    other = 1 - core
    sign = 1 - 2 * core
    nodes = X_HI * nz * CORES

    def dev(xh, xl, y, z, core):
        return (xh * (nz * CORES) + z * CORES + core, y * X_LO + xl)

    def along_y(step, on_core):
        return dev(xh, xl, lax.rem(y + step + NY, NY), z, on_core)

    mate = dev(xh, xl, y, z, other)
    across = dev(lax.rem(xh + core, X_HI), 1 - xl, y, z, core)
    y_fwd, y_bwd, y_bwd2 = along_y(sign, core), along_y(-sign, core), along_y(-2 * sign, core)
    nxt = (lax.rem(node + 1, nodes), rep)
    prv = (lax.rem(node + nodes - 1, nodes), rep)
    my_piece = xh * Z_IN + zi
    scatter_peers = []
    for j in range(1, npiece):
        pxh = lax.rem(xh + j // Z_IN, X_HI)
        pzi = lax.rem(zi + j % Z_IN, Z_IN)
        scatter_peers.append((j, dev(pxh, xl, y, zg * Z_IN + pzi, core), pxh * Z_IN + pzi))
    tri_peers = []
    for j in range(1, zg_n):
        tri_peers.append((j, dev(xh, xl, y, lax.rem(zg + j, zg_n) * Z_IN + zi, core)))

    barrier = pltpu.get_barrier_semaphore()
    peers = [mate, across, y_fwd, y_bwd, along_y(sign, other), along_y(-sign, other)]
    peers += [along_y(2, core), along_y(-2, core), along_y(HALF, core), along_y(HALF, other), nxt, prv]
    peers += [d for _, d, _ in scatter_peers] + [d for _, d in tri_peers]
    for peer in peers:
        pl.semaphore_signal(barrier, inc=1, device_id=peer, device_id_type=MESH)

    own, by_mate, by_x, by_x_mate = [pl.ds(k * nrow, nrow) for k in range(4)]
    near, far = pl.ds(0, 2 * nrow), pl.ds(2 * nrow, 2 * nrow)
    loads = [
        pltpu.make_async_copy(agg_ref, rows_a.at[own], l_sem.at[0]),
        pltpu.make_async_copy(cot_ref, rows_c.at[own], l_sem.at[1]),
        pltpu.make_async_copy(tiles_ref.at[0], tiles, l_sem.at[2]),
    ]
    shard_loads = [
        pltpu.make_async_copy(kin_ref, w_in.at[0], l_sem.at[3]),
        pltpu.make_async_copy(kout_ref, w_out.at[0], l_sem.at[4]),
    ]
    for load in loads:
        load.start()

    @pl.when(core == 0)
    def _():
        for load in shard_loads:
            load.start()

    pl.semaphore_wait(barrier, len(peers))

    started = []
    used = [0]

    def ids(count=1):
        used[0] += count
        return used[0] - count

    def copy_to(src, dst, k, device, k_recv=None):
        return pltpu.make_async_remote_copy(
            src_ref=src, dst_ref=dst, send_sem=s_sem.at[k], recv_sem=r_sem.at[k if k_recv is None else k_recv],
            device_id=device, device_id_type=MESH,
        )

    def send(src, dst, k, device, k_recv=None):
        copy = copy_to(src, dst, k, device, k_recv)
        copy.start()
        started.append(copy)

    def arrive(dst, k):
        copy_to(dst, dst, k, mate).wait_recv()

    k_win, k_wout = ids(HALF), ids(HALF)
    k_anti_in, k_anti_out = ids(), ids()
    k_mate_rows, k_x_rows, k_fwd_rows = ids(2), ids(2), ids(2)
    k_mid = ids(4)
    k_fin, k_fin_anti, k_fin_mate = ids(4), ids(2), ids()
    k_back = ids(3)
    k_halo = ids(2)
    k_piece, k_tri, k_tot, k_swap = ids(npiece), ids(zg_n), ids(npiece), ids()
    assert used[0] <= N_SEM

    send(kin_ref, w_in.at[1], k_win + 1, y_fwd)
    send(kout_ref, w_out.at[1], k_wout + 1, y_fwd)
    send(agg_ref, rows_a.at[by_x], k_x_rows, across)
    send(cot_ref, rows_c.at[by_x], k_x_rows + 1, across)
    send(agg_ref, rows_a.at[by_mate], k_mate_rows, mate)
    send(cot_ref, rows_c.at[by_mate], k_mate_rows + 1, mate)
    opposite = along_y(HALF, core)
    anti_in = copy_to(kin_ref, w_in.at[0], k_anti_in, opposite)
    anti_out = copy_to(kout_ref, w_out.at[0], k_anti_out, opposite)

    @pl.when(core == 1)
    def _():
        anti_in.start()
        anti_out.start()

    acc[...] = jnp.zeros_like(acc)
    for load in loads:
        load.wait()

    def flip(block):
        at[:, block] = rows_a[block].T
        ct[:, block] = rows_c[block].T

    flip(own)
    arrive(rows_a.at[by_mate], k_mate_rows)
    arrive(rows_c.at[by_mate], k_mate_rows + 1)
    flip(by_mate)
    for t in range(tiles.shape[0]):
        tiles[t] = tiles[t].T

    def pass_on(j, last):
        for buf, k in ((w_in, k_win), (w_out, k_wout)):
            arrive(buf.at[j], k + j)
            if not last:
                send(buf.at[j], buf.at[j + 1], k + j + 1, y_fwd)

    def unit(j, rows):
        a, g = gelu_pair(dot(rows_a[rows], w_in[j]), dot_last(rows_c[rows], w_out[j]))
        act[j, rows] = a
        gpre[j, rows] = g

    def add_agg(j, rows):
        acc[rows] += dot_last(gpre[j, rows], w_in[j])

    def weight_terms(j):
        return dot(at[...], gpre[j]), dot(ct[...], act[j])

    pass_on(1, False)
    unit(1, near)
    add_agg(1, near)
    arrive(rows_a.at[by_x], k_x_rows)
    send(rows_a.at[by_x], rows_a.at[by_x_mate], k_fwd_rows, mate)
    pass_on(2, False)
    arrive(rows_c.at[by_x], k_x_rows + 1)
    send(rows_c.at[by_x], rows_c.at[by_x_mate], k_fwd_rows + 1, mate)
    flip(by_x)
    unit(2, near)
    add_agg(2, near)
    arrive(rows_a.at[by_x_mate], k_fwd_rows)
    arrive(rows_c.at[by_x_mate], k_fwd_rows + 1)
    flip(by_x_mate)
    unit(2, far)
    terms = weight_terms(2)
    for m in range(2):
        part[2, m] = terms[m].astype(BF16)
        send(part.at[2, m], mid_in.at[0, m], k_mid + m, y_bwd)
    add_agg(2, far)
    unit(1, far)
    terms = weight_terms(1)
    for m in range(2):
        first[m] = terms[m]
    add_agg(1, far)

    @pl.when(core == 0)
    def _():
        for load in shard_loads:
            load.wait()

    @pl.when(core == 1)
    def _():
        arrive(w_in.at[0], k_anti_in)
        arrive(w_out.at[0], k_anti_out)

    unit(0, near)
    unit(0, far)
    terms = weight_terms(0)
    for m in range(2):
        part[0, m] = terms[m].astype(BF16)
    own_to_mate = copy_to(part.at[0, 1], fin_in.at[3], k_fin_mate, mate)
    to_opposite = [
        copy_to(part.at[0, m], fin_in.at[2], k_fin_anti + m, along_y(HALF, m), k_fin_anti) for m in range(2)
    ]

    @pl.when(core == 0)
    def _():
        own_to_mate.start()
        fin_in[3] = part[0, 0]

    @pl.when(core == 1)
    def _():
        for copy in to_opposite:
            copy.start()

    add_agg(0, near)
    add_agg(0, far)
    pass_on(3, True)
    unit(3, near)
    unit(3, far)
    terms = weight_terms(3)
    for m in range(2):
        part[3, m] = terms[m].astype(BF16)
        send(part.at[3, m], mid_in.at[1, m], k_mid + 2 + m, y_bwd2)
    add_agg(3, near)
    add_agg(3, far)

    back_out[0] = acc[by_mate].astype(BF16)
    back_out[1] = acc[by_x_mate].astype(BF16)
    send(back_out.at[0], back_in.at[0], k_back, mate)
    send(back_out.at[1], back_in.at[1], k_back + 1, mate)

    for m in range(2):
        arrive(mid_in.at[0, m], k_mid + m)
        arrive(mid_in.at[1, m], k_mid + 2 + m)
        first_out[m] = (first[m] + mid_in[0, m].astype(F32) + mid_in[1, m].astype(F32)).astype(BF16)
        send(first_out.at[m], fin_in.at[core], k_fin + 2 * m, along_y(-sign, m), k_fin + core)

    arrive(back_in.at[1], k_back + 1)
    back_out[2] = (acc[by_x] + back_in[1].astype(F32)).astype(BF16)
    send(back_out.at[2], back_in.at[2], k_back + 2, across)

    arrive(fin_in.at[2], k_fin_anti)

    @pl.when(core == 1)
    def _():
        arrive(fin_in.at[3], k_fin_mate)

    mine = fin_in[3].astype(F32) + fin_in[2].astype(F32)
    for c in range(2):
        arrive(fin_in.at[c], k_fin + c)
        mine = mine + fin_in[c].astype(F32)

    prow = feat // npiece
    for p in range(npiece):
        pieces[p] = mine[p * prow : (p + 1) * prow].astype(BF16)
    for j, peer, p in scatter_peers:
        send(pieces.at[p], piece_in.at[j], k_piece + j, peer)

    arrive(back_in.at[0], k_back)
    arrive(back_in.at[2], k_back + 2)
    g_agg = (acc[own] + back_in[0].astype(F32) + back_in[2].astype(F32)).astype(BF16)
    live_count = count_ref[0]
    sums = [None, None, None]
    for t in range(tiles.shape[0]):
        term = dot(tiles[t], g_agg)
        for k in range(3):
            on = jnp.logical_and(cols_ref[0, t] == k, t < live_count)
            add = term * jnp.where(on, 1.0, 0.0).astype(F32)
            sums[k] = add if sums[k] is None else sums[k] + add
    halo_out[0] = sums[0].astype(BF16)
    halo_out[1] = sums[2].astype(BF16)
    acc[own] = sums[1] + rows_c[own].astype(F32)
    send(halo_out.at[0], halo_in.at[0], k_halo, prv)
    send(halo_out.at[1], halo_in.at[1], k_halo + 1, nxt)

    tot = pieces[my_piece].astype(F32)
    for j, peer, _ in scatter_peers:
        arrive(piece_in.at[j], k_piece + j)
        tot = tot + piece_in[j].astype(F32)
    triple[...] = tot.astype(BF16)
    for j, peer in tri_peers:
        send(triple, triple_in.at[zg], k_tri + j, peer)
    triple_in[zg] = triple[...]

    arrive(halo_in.at[0], k_halo)
    arrive(halo_in.at[1], k_halo + 1)
    nodes_ref[...] = (acc[own] + halo_in[1].astype(F32) + halo_in[0].astype(F32)).astype(BF16)

    for j, peer in tri_peers:
        arrive(triple_in.at[lax.rem(zg + zg_n - j, zg_n)], k_tri + j)
    tot = triple_in[0].astype(F32)
    for k in range(1, zg_n):
        tot = tot + triple_in[k].astype(F32)
    total[core, my_piece] = tot.astype(BF16)
    for j, peer, _ in scatter_peers:
        send(total.at[core, my_piece], total.at[core, my_piece], k_tot + j, peer)
    for j, peer, _ in scatter_peers:
        fxh = lax.rem(xh + X_HI - j // Z_IN, X_HI)
        fzi = lax.rem(zi + Z_IN - j % Z_IN, Z_IN)
        arrive(total.at[core, fxh * Z_IN + fzi], k_tot + j)
    send(total.at[core], total.at[core], k_swap, mate)
    arrive(total.at[other], k_swap)
    for p in range(npiece):
        gin_ref[p * prow : (p + 1) * prow, :] = total[0, p]
    gout_ref[...] = jnp.concatenate([total[1, p] for p in range(npiece)], axis=0).T
    for copy in started:
        copy.wait_send()

    @pl.when(core == 0)
    def _():
        own_to_mate.wait_send()

    @pl.when(core == 1)
    def _():
        anti_in.wait_send()
        anti_out.wait_send()
        for copy in to_opposite:
            copy.wait_send()


def local(nz, aggregated, cotangent, kernel_in, kernel_out, tile_values, tile_cols, tile_count):
    nrow, feat = aggregated.shape
    assert lax.axis_size("rep") == NY * X_LO
    hid = kernel_in.shape[1]
    slots = tile_values.shape[1]
    npiece = X_HI * Z_IN
    zg_n = nz // Z_IN
    prow = feat // npiece
    norm_factor = 1.0 / math.sqrt(nrow * lax.axis_size("node") * lax.axis_size("rep"))
    vmem = lambda shape, dtype=BF16: pltpu.VMEM(shape, dtype)
    full = pl.BlockSpec(memory_space=pltpu.VMEM)
    hbm = pl.BlockSpec(memory_space=pltpu.HBM)
    scalars = pl.BlockSpec(memory_space=pltpu.SMEM)
    grad_nodes, g_in, g_out = pl.pallas_call(
        functools.partial(kernel, nz),
        out_shape=(
            jax.ShapeDtypeStruct((nrow, feat), BF16),
            jax.ShapeDtypeStruct((feat, hid), BF16),
            jax.ShapeDtypeStruct((hid, feat), BF16),
        ),
        in_specs=[hbm] * 5 + [scalars] * 2,
        out_specs=(full, full, full),
        scratch_shapes=[
            vmem((4 * nrow, feat)),
            vmem((4 * nrow, feat)),
            vmem((feat, 4 * nrow)),
            vmem((feat, 4 * nrow)),
            vmem((slots, nrow, nrow)),
            vmem((HALF, feat, hid)),
            vmem((HALF, hid, feat)),
            vmem((HALF, 4 * nrow, hid)),
            vmem((HALF, 4 * nrow, hid)),
            vmem((HALF, 2, feat, hid)),
            vmem((2, feat, hid), F32),
            vmem((2, feat, hid)),
            vmem((2, 2, feat, hid)),
            vmem((4, feat, hid)),
            vmem((4 * nrow, feat), F32),
            vmem((3, nrow, feat)),
            vmem((3, nrow, feat)),
            vmem((2, nrow, feat)),
            vmem((2, nrow, feat)),
            vmem((npiece, prow, hid)),
            vmem((npiece, prow, hid)),
            vmem((prow, hid)),
            vmem((zg_n, prow, hid)),
            vmem((2, npiece, prow, hid)),
            pltpu.SemaphoreType.DMA((N_SEM,)),
            pltpu.SemaphoreType.DMA((N_SEM,)),
            pltpu.SemaphoreType.DMA((5,)),
        ],
        compiler_params=pltpu.CompilerParams(
            collective_id=0, has_side_effects=True, vmem_limit_bytes=62 << 20
        ),
    )(aggregated, cotangent, kernel_in, kernel_out, tile_values, tile_cols, tile_count)
    return (grad_nodes, g_in.astype(F32) * norm_factor, g_out.astype(F32) * norm_factor)


def solution(mesh):
    nz = mesh.shape["node"] // (X_HI * CORES)
    return jax.shard_map(
        functools.partial(local, nz),
        mesh=mesh,
        in_specs=(
            P(("node", "rep"), None),
            P(("node", "rep"), None),
            P(None, "rep"),
            P("rep", None),
            P(("node", "rep"), None, None, None),
            P(("node", "rep"), None),
            P(("node", "rep")),
        ),
        out_specs=(P(("node", "rep"), None), P(None, "rep"), P("rep", None)),
        check_vma=False,
    )
```

```python
import functools
import math

import jax
import jax.numpy as jnp
from jax import lax
from jax.experimental import pallas as pl
from jax.experimental.pallas import tpu as pltpu
from jax.sharding import PartitionSpec as P

MESH = pl.DeviceIdType.MESH
BF16 = jnp.bfloat16
F32 = jnp.float32
X_HI, X_LO, CORES, NY, Z_IN = 2, 2, 2, 8, 4
HALF = NY // 2
GELU_C = math.sqrt(2.0 / math.pi)
N_SEM = 64


def dot(left, right):
    return jnp.dot(left, right, preferred_element_type=F32)


def dot_last(left, right):
    return lax.dot_general(left, right, (((1,), (1,)), ((), ())), preferred_element_type=F32)


def gelu_pair(pre, g_act):
    sq = pre * pre
    th = jnp.tanh(GELU_C * (pre + 0.044715 * sq * pre))
    half = 0.5 * (1.0 + th)
    slope = half + 0.5 * pre * (1.0 - th * th) * GELU_C * (1.0 + 3.0 * 0.044715 * sq)
    return (pre * half).astype(BF16), (g_act * slope).astype(BF16)


def kernel(
    nz, norm_factor,
    agg_ref, cot_ref, kin_ref, kout_ref, tiles_ref, cols_ref, count_ref,
    nodes_ref, gin_ref, gout_ref,
    rows_a, rows_c, at, ct, tiles, w_in, w_out, act, gpre, part, chain_out, chain_in, anti_out, fin_in,
    acc, back_out, back_in, halo_out, halo_in, pieces, piece_in, triple, triple_in, total,
    nodes_buf, gin_buf, gout_buf,
    s_sem, r_sem, l_sem,
):
    zg_n = nz // Z_IN
    npiece = X_HI * Z_IN
    nrow, feat = agg_ref.shape
    hid = kin_ref.shape[1]
    node, rep = lax.axis_index("node"), lax.axis_index("rep")
    core = lax.rem(node, CORES)
    z = lax.rem(lax.div(node, CORES), nz)
    xh = lax.div(node, CORES * nz)
    y, xl = lax.div(rep, X_LO), lax.rem(rep, X_LO)
    zg, zi = lax.div(z, Z_IN), lax.rem(z, Z_IN)
    other = 1 - core
    sign = 1 - 2 * core
    nodes = X_HI * nz * CORES

    def dev(xh, xl, y, z, core):
        return (xh * (nz * CORES) + z * CORES + core, y * X_LO + xl)

    def along_y(step, on_core):
        return dev(xh, xl, lax.rem(y + step + NY, NY), z, on_core)

    mate = dev(xh, xl, y, z, other)
    across = dev(lax.rem(xh + core, X_HI), 1 - xl, y, z, core)
    y_fwd, y_bwd = along_y(sign, core), along_y(-sign, core)
    nxt = (lax.rem(node + 1, nodes), rep)
    prv = (lax.rem(node + nodes - 1, nodes), rep)
    my_piece = xh * Z_IN + zi
    scatter_peers = []
    for j in range(1, npiece):
        pxh = lax.rem(xh + j // Z_IN, X_HI)
        pzi = lax.rem(zi + j % Z_IN, Z_IN)
        scatter_peers.append((j, dev(pxh, xl, y, zg * Z_IN + pzi, core), pxh * Z_IN + pzi))
    tri_peers = []
    for j in range(1, zg_n):
        tri_peers.append((j, dev(xh, xl, y, lax.rem(zg + j, zg_n) * Z_IN + zi, core)))

    barrier = pltpu.get_barrier_semaphore()
    peers = [y_fwd, y_bwd, across, mate, along_y(sign, other), along_y(-sign, other)]
    peers += [along_y(HALF, core), along_y(HALF, other), nxt, prv]
    peers += [d for _, d, _ in scatter_peers] + [d for _, d in tri_peers]
    for peer in peers:
        pl.semaphore_signal(barrier, inc=1, device_id=peer, device_id_type=MESH)

    def in_slot(slot):
        start = slot * hid
        return pl.ds(start if isinstance(slot, int) else pl.multiple_of(start, hid), hid)

    own, by_mate, by_x, by_x_mate = [pl.ds(k * nrow, nrow) for k in range(4)]
    near, far = pl.ds(0, 2 * nrow), pl.ds(2 * nrow, 2 * nrow)
    every = pl.ds(0, 4 * nrow)
    loads = [
        pltpu.make_async_copy(agg_ref, rows_a.at[own], l_sem.at[0]),
        pltpu.make_async_copy(cot_ref, rows_c.at[own], l_sem.at[1]),
        pltpu.make_async_copy(tiles_ref.at[0], tiles, l_sem.at[2]),
    ]
    shard_loads = [
        pltpu.make_async_copy(kin_ref, w_in.at[:, in_slot(0)], l_sem.at[3]),
        pltpu.make_async_copy(kout_ref, w_out.at[in_slot(0)], l_sem.at[4]),
    ]
    for load in loads:
        load.start()

    @pl.when(core == 0)
    def _():
        for load in shard_loads:
            load.start()

    pl.semaphore_wait(barrier, len(peers))

    started = []
    started_on = ([], [])
    used = [0]

    def ids(count=1):
        used[0] += count
        return used[0] - count

    def copy_to(src, dst, k, device, k_recv=None):
        return pltpu.make_async_remote_copy(
            src_ref=src, dst_ref=dst, send_sem=s_sem.at[k], recv_sem=r_sem.at[k if k_recv is None else k_recv],
            device_id=device, device_id_type=MESH,
        )

    def send(src, dst, k, device, k_recv=None):
        copy = copy_to(src, dst, k, device, k_recv)
        copy.start()
        started.append(copy)

    def send_on(only, make):
        make().start()
        started_on[only].append(make)

    def arrive(dst, k):
        copy_to(dst, dst, k, mate).wait_recv()

    k_win, k_wout = ids(HALF + 1), ids(HALF + 1)
    k_mate_rows, k_x_rows, k_fwd_rows = ids(2), ids(2), ids(2)
    k_chain = ids(2 * HALF)
    k_fin, k_fin_anti, k_fin_mate = ids(4), ids(2), ids()
    k_back = ids(3)
    k_halo = ids(2)
    k_piece, k_tri, k_tot, k_swap = ids(npiece), ids(zg_n), ids(npiece), ids()
    assert used[0] <= N_SEM

    def w_at(m, slot):
        return w_in.at[:, in_slot(slot)] if m == 0 else w_out.at[in_slot(slot)]

    def arrive_shard(m, j):
        arrive(w_at(m, j - core), (k_win, k_wout)[m] + j)

    def forward_shard(m, j):
        send(w_at(m, j - core), w_at(m, j + 1 - core), (k_win, k_wout)[m] + j + 1, y_fwd)

    send(kin_ref, w_at(0, other), k_win + 1, y_fwd)
    send(kout_ref, w_at(1, other), k_wout + 1, y_fwd)
    send(agg_ref, rows_a.at[by_x], k_x_rows, across)
    send(cot_ref, rows_c.at[by_x], k_x_rows + 1, across)
    send(agg_ref, rows_a.at[by_mate], k_mate_rows, mate)
    send(cot_ref, rows_c.at[by_mate], k_mate_rows + 1, mate)

    def flip(block):
        at[:, block] = rows_a[block].T
        ct[:, block] = rows_c[block].T

    def unit(slot, rows):
        a, g = gelu_pair(dot(rows_a[rows], w_in[:, in_slot(slot)]), dot_last(rows_c[rows], w_out[in_slot(slot)]))
        act[rows, in_slot(slot)] = a
        gpre[rows, in_slot(slot)] = g

    def weight_terms(slot, count=1):
        cols = pl.ds(slot * hid, count * hid)
        terms = (dot(at[...], gpre[:, cols]), dot(ct[...], act[:, cols]))
        for m in range(2):
            for k in range(count):
                part[slot + k, m] = terms[m][:, k * hid : (k + 1) * hid]

    for load in loads:
        load.wait()
    flip(own)
    arrive(rows_a.at[by_mate], k_mate_rows)
    arrive(rows_c.at[by_mate], k_mate_rows + 1)
    flip(by_mate)
    for m in range(2):
        arrive_shard(m, 1)
        forward_shard(m, 1)

    @pl.when(core == 0)
    def _():
        for load in shard_loads:
            load.wait()

    arrive(rows_a.at[by_x], k_x_rows)
    send(rows_a.at[by_x], rows_a.at[by_x_mate], k_fwd_rows, mate)
    unit(0, near)
    for m in range(2):
        arrive_shard(m, 2)
        forward_shard(m, 2)
    arrive(rows_c.at[by_x], k_x_rows + 1)
    send(rows_c.at[by_x], rows_c.at[by_x_mate], k_fwd_rows + 1, mate)
    unit(1, near)
    flip(by_x)
    arrive(rows_a.at[by_x_mate], k_fwd_rows)
    arrive(rows_c.at[by_x_mate], k_fwd_rows + 1)
    unit(0, far)
    unit(1, far)
    flip(by_x_mate)
    weight_terms(0, 2)

    @pl.when(core == 0)
    def _():
        anti_out[1] = part[0, 1].astype(BF16)
        send_on(0, lambda: copy_to(anti_out.at[1], fin_in.at[3], k_fin_mate, mate))

    def chain_start(only):
        for m in range(2):
            chain_out[HALF - 1, m] = part[HALF - 1 - only, m].astype(BF16)
            send_on(only, lambda m=m: copy_to(chain_out.at[HALF - 1, m], chain_in.at[HALF - 1, m], k_chain + 2 * (HALF - 1) + m, y_bwd))

    for m in range(2):
        arrive_shard(m, 3)

        @pl.when(core == 1)
        def _():
            send_on(1, lambda m=m: copy_to(w_at(m, 2), w_at(m, 3), (k_win, k_wout)[m] + HALF, y_fwd))

    unit(2, every)
    weight_terms(2)

    @pl.when(core == 1)
    def _():
        chain_start(1)
        for m in range(2):
            arrive(w_at(m, 3), (k_win, k_wout)[m] + HALF)

    unit(3, every)
    weight_terms(3)

    @pl.when(core == 0)
    def _():
        chain_start(0)

    @pl.when(core == 1)
    def _():
        for m in range(2):
            anti_out[m] = part[3, m].astype(BF16)
            send_on(1, lambda m=m: copy_to(anti_out.at[m], fin_in.at[2], k_fin_anti + m, along_y(HALF, m), k_fin_anti))

    def shares(block):
        return dot_last(gpre[block], w_in[...])

    def chain_step(k, m):
        arrive(chain_in.at[k + 1, m], k_chain + 2 * (k + 1) + m)
        chain_out[k, m] = (part[k - core, m] + chain_in[k + 1, m].astype(F32)).astype(BF16)
        if k > 1:
            send(chain_out.at[k, m], chain_in.at[k, m], k_chain + 2 * k + m, y_bwd)
        else:
            send(chain_out.at[k, m], fin_in.at[core], k_fin + 2 * m, along_y(-sign, m), k_fin + core)

    back_out[1] = shares(by_x_mate).astype(BF16)
    send(back_out.at[1], back_in.at[1], k_back + 1, mate)
    back_out[0] = shares(by_mate).astype(BF16)
    send(back_out.at[0], back_in.at[0], k_back, mate)
    for m in range(2):
        chain_step(2, m)
    acc[...] = shares(by_x)
    arrive(back_in.at[1], k_back + 1)
    back_out[2] = (acc[...] + back_in[1].astype(F32)).astype(BF16)
    send(back_out.at[2], back_in.at[2], k_back + 2, across)
    acc[...] = shares(own)
    for t in range(tiles.shape[0]):
        tiles[t] = tiles[t].T
    for m in range(2):
        chain_step(1, m)

    @pl.when(core == 1)
    def _():
        arrive(fin_in.at[3], k_fin_mate)

    @pl.when(core == 0)
    def _():
        fin_in[3] = part[0, 0].astype(BF16)

    arrive(fin_in.at[2], k_fin_anti)
    mine = fin_in[3].astype(F32) + fin_in[2].astype(F32)
    for c in range(2):
        arrive(fin_in.at[c], k_fin + c)
        mine = mine + fin_in[c].astype(F32)

    prow = feat // npiece
    for p in range(npiece):
        pieces[p] = mine[p * prow : (p + 1) * prow].astype(BF16)
    for j, peer, p in scatter_peers:
        send(pieces.at[p], piece_in.at[j], k_piece + j, peer)

    arrive(back_in.at[0], k_back)
    arrive(back_in.at[2], k_back + 2)
    g_agg = (acc[...] + back_in[0].astype(F32) + back_in[2].astype(F32)).astype(BF16)
    live_count = count_ref[0]
    sums = [None, None, None]
    for t in range(tiles.shape[0]):
        term = dot(tiles[t], g_agg)
        for k in range(3):
            on = jnp.logical_and(cols_ref[0, t] == k, t < live_count)
            add = term * jnp.where(on, 1.0, 0.0).astype(F32)
            sums[k] = add if sums[k] is None else sums[k] + add
    halo_out[0] = sums[0].astype(BF16)
    halo_out[1] = sums[2].astype(BF16)
    acc[...] = sums[1] + rows_c[own].astype(F32)
    send(halo_out.at[0], halo_in.at[0], k_halo, prv)
    send(halo_out.at[1], halo_in.at[1], k_halo + 1, nxt)

    tot = pieces[my_piece].astype(F32)
    for j, peer, _ in scatter_peers:
        arrive(piece_in.at[j], k_piece + j)
        tot = tot + piece_in[j].astype(F32)
    triple[...] = tot.astype(BF16)
    for j, peer in tri_peers:
        send(triple, triple_in.at[zg], k_tri + j, peer)
    triple_in[zg] = triple[...]

    arrive(halo_in.at[0], k_halo)
    arrive(halo_in.at[1], k_halo + 1)
    nodes_buf[...] = (acc[...] + halo_in[1].astype(F32) + halo_in[0].astype(F32)).astype(BF16)
    out_nodes = pltpu.make_async_copy(nodes_buf, nodes_ref, l_sem.at[0])
    out_nodes.start()

    for j, peer in tri_peers:
        arrive(triple_in.at[lax.rem(zg + zg_n - j, zg_n)], k_tri + j)
    tot = triple_in[0].astype(F32)
    for k in range(1, zg_n):
        tot = tot + triple_in[k].astype(F32)
    total[core, my_piece] = tot.astype(BF16)
    for j, peer, _ in scatter_peers:
        send(total.at[core, my_piece], total.at[core, my_piece], k_tot + j, peer)
    for j, peer, _ in scatter_peers:
        fxh = lax.rem(xh + X_HI - j // Z_IN, X_HI)
        fzi = lax.rem(zi + Z_IN - j % Z_IN, Z_IN)
        arrive(total.at[core, fxh * Z_IN + fzi], k_tot + j)
    send(total.at[core], total.at[core], k_swap, mate)
    arrive(total.at[other], k_swap)
    for p in range(npiece):
        gin_buf[p * prow : (p + 1) * prow, :] = total[0, p].astype(F32) * norm_factor
    out_gin = pltpu.make_async_copy(gin_buf, gin_ref, l_sem.at[1])
    out_gin.start()
    gout_buf[...] = jnp.concatenate([total[1, p] for p in range(npiece)], axis=0).T.astype(F32) * norm_factor
    out_gout = pltpu.make_async_copy(gout_buf, gout_ref, l_sem.at[2])
    out_gout.start()
    for copy in started:
        copy.wait_send()
    for only in range(2):

        @pl.when(core == only)
        def _():
            for make in started_on[only]:
                make().wait_send()

    out_nodes.wait()
    out_gin.wait()
    out_gout.wait()


def hand_over(*refs):
    n = len(refs) // 2
    copies = [pltpu.make_async_copy(refs[k], refs[n + k], refs[-1].at[k]) for k in range(n)]
    for copy in copies:
        copy.start()
    for copy in copies:
        copy.wait()


def local(nz, aggregated, cotangent, kernel_in, kernel_out, tile_values, tile_cols, tile_count):
    nrow, feat = aggregated.shape
    assert lax.axis_size("rep") == NY * X_LO
    hid = kernel_in.shape[1]
    slots = tile_values.shape[1]
    npiece = X_HI * Z_IN
    zg_n = nz // Z_IN
    prow = feat // npiece
    norm_factor = 1.0 / math.sqrt(nrow * lax.axis_size("node") * lax.axis_size("rep"))
    vmem = lambda shape, dtype=BF16: pltpu.VMEM(shape, dtype)
    hbm = pl.BlockSpec(memory_space=pltpu.HBM)
    scalars = pl.BlockSpec(memory_space=pltpu.SMEM)
    shapes = (
        jax.ShapeDtypeStruct((nrow, feat), BF16),
        jax.ShapeDtypeStruct((feat, hid), F32),
        jax.ShapeDtypeStruct((hid, feat), F32),
    )
    results = pl.pallas_call(
        functools.partial(kernel, nz, norm_factor),
        out_shape=shapes,
        in_specs=[hbm] * 5 + [scalars] * 2,
        out_specs=(hbm, hbm, hbm),
        scratch_shapes=[
            vmem((4 * nrow, feat)),
            vmem((4 * nrow, feat)),
            vmem((feat, 4 * nrow)),
            vmem((feat, 4 * nrow)),
            vmem((slots, nrow, nrow)),
            vmem((feat, HALF * hid)),
            vmem((HALF * hid, feat)),
            vmem((4 * nrow, HALF * hid)),
            vmem((4 * nrow, HALF * hid)),
            vmem((HALF, 2, feat, hid), F32),
            vmem((HALF, 2, feat, hid)),
            vmem((HALF, 2, feat, hid)),
            vmem((2, feat, hid)),
            vmem((4, feat, hid)),
            vmem((nrow, feat), F32),
            vmem((3, nrow, feat)),
            vmem((3, nrow, feat)),
            vmem((2, nrow, feat)),
            vmem((2, nrow, feat)),
            vmem((npiece, prow, hid)),
            vmem((npiece, prow, hid)),
            vmem((prow, hid)),
            vmem((zg_n, prow, hid)),
            vmem((2, npiece, prow, hid)),
            vmem((nrow, feat)),
            vmem((feat, hid), F32),
            vmem((hid, feat), F32),
            pltpu.SemaphoreType.DMA((N_SEM,)),
            pltpu.SemaphoreType.DMA((N_SEM,)),
            pltpu.SemaphoreType.DMA((5,)),
        ],
        compiler_params=pltpu.CompilerParams(
            collective_id=0, has_side_effects=True, vmem_limit_bytes=62 << 20
        ),
    )(aggregated, cotangent, kernel_in, kernel_out, tile_values, tile_cols, tile_count)
    return pl.pallas_call(
        hand_over,
        out_shape=shapes,
        in_specs=[hbm] * 3,
        out_specs=(hbm, hbm, hbm),
        scratch_shapes=[pltpu.SemaphoreType.DMA((3,))],
        compiler_params=pltpu.CompilerParams(vmem_limit_bytes=62 << 20),
    )(*results)


def solution(mesh):
    nz = mesh.shape["node"] // (X_HI * CORES)
    return jax.shard_map(
        functools.partial(local, nz),
        mesh=mesh,
        in_specs=(
            P(("node", "rep"), None),
            P(("node", "rep"), None),
            P(None, "rep"),
            P("rep", None),
            P(("node", "rep"), None, None, None),
            P(("node", "rep"), None),
            P(("node", "rep")),
        ),
        out_specs=(P(("node", "rep"), None), P(None, "rep"), P("rep", None)),
        check_vma=False,
    )
```

```python
import functools
import math

import jax
import jax.numpy as jnp
from jax import lax
from jax.experimental import pallas as pl
from jax.experimental.pallas import tpu as pltpu
from jax.sharding import PartitionSpec as P

MESH = pl.DeviceIdType.MESH
BF16 = jnp.bfloat16
F32 = jnp.float32
X_HI, X_LO, CORES, NY, Z_IN = 2, 2, 2, 8, 4
HALF = NY // 2
GELU_C = math.sqrt(2.0 / math.pi)
N_SEM = 64


def dot(left, right):
    return jnp.dot(left, right, preferred_element_type=F32)


def dot_last(left, right):
    return lax.dot_general(left, right, (((1,), (1,)), ((), ())), preferred_element_type=F32)


def gelu_pair(pre, g_act):
    sq = pre * pre
    th = jnp.tanh(GELU_C * (pre + 0.044715 * sq * pre))
    half = 0.5 * (1.0 + th)
    slope = half + 0.5 * pre * (1.0 - th * th) * GELU_C * (1.0 + 3.0 * 0.044715 * sq)
    return (pre * half).astype(BF16), (g_act * slope).astype(BF16)


def kernel(
    nz, norm_factor,
    agg_ref, cot_ref, kin_ref, kout_ref, tiles_ref, cols_ref, count_ref,
    nodes_ref, gin_ref, gout_ref,
    rows_a, rows_c, at, ct, tiles, w_in, w_out, act, gpre, part, chain_out, chain_in, anti_out, fin_in,
    acc, back_out, back_in, halo_out, halo_in, pieces, piece_in, triple, triple_in, total,
    nodes_buf, gin_buf, gout_buf,
    s_sem, r_sem, l_sem,
):
    zg_n = nz // Z_IN
    npiece = X_HI * Z_IN
    nrow, feat = agg_ref.shape
    hid = kin_ref.shape[1]
    node, rep = lax.axis_index("node"), lax.axis_index("rep")
    core = lax.rem(node, CORES)
    z = lax.rem(lax.div(node, CORES), nz)
    xh = lax.div(node, CORES * nz)
    y, xl = lax.div(rep, X_LO), lax.rem(rep, X_LO)
    zg, zi = lax.div(z, Z_IN), lax.rem(z, Z_IN)
    other = 1 - core
    sign = 1 - 2 * core
    nodes = X_HI * nz * CORES

    def dev(xh, xl, y, z, core):
        return (xh * (nz * CORES) + z * CORES + core, y * X_LO + xl)

    def along_y(step, on_core):
        return dev(xh, xl, lax.rem(y + step + NY, NY), z, on_core)

    mate = dev(xh, xl, y, z, other)
    across = dev(lax.rem(xh + core, X_HI), 1 - xl, y, z, core)
    y_fwd, y_bwd = along_y(sign, core), along_y(-sign, core)
    nxt = (lax.rem(node + 1, nodes), rep)
    prv = (lax.rem(node + nodes - 1, nodes), rep)
    my_piece = xh * Z_IN + zi
    scatter_peers = []
    for j in range(1, npiece):
        pxh = lax.rem(xh + j // Z_IN, X_HI)
        pzi = lax.rem(zi + j % Z_IN, Z_IN)
        scatter_peers.append((j, dev(pxh, xl, y, zg * Z_IN + pzi, core), pxh * Z_IN + pzi))
    tri_peers = []
    for j in range(1, zg_n):
        tri_peers.append((j, dev(xh, xl, y, lax.rem(zg + j, zg_n) * Z_IN + zi, core)))

    barrier = pltpu.get_barrier_semaphore()
    peers = [y_fwd, y_bwd, across, mate, along_y(sign, other), along_y(-sign, other)]
    peers += [along_y(HALF, core), along_y(HALF, other), nxt, prv]
    peers += [d for _, d, _ in scatter_peers] + [d for _, d in tri_peers]
    for peer in peers:
        pl.semaphore_signal(barrier, inc=1, device_id=peer, device_id_type=MESH)

    def in_slot(slot):
        start = slot * hid
        return pl.ds(start if isinstance(slot, int) else pl.multiple_of(start, hid), hid)

    own, by_mate, by_x, by_x_mate = [pl.ds(k * nrow, nrow) for k in range(4)]
    near, far = pl.ds(0, 2 * nrow), pl.ds(2 * nrow, 2 * nrow)
    every = pl.ds(0, 4 * nrow)
    loads = [
        pltpu.make_async_copy(agg_ref, rows_a.at[own], l_sem.at[0]),
        pltpu.make_async_copy(cot_ref, rows_c.at[own], l_sem.at[1]),
        pltpu.make_async_copy(tiles_ref.at[0], tiles, l_sem.at[2]),
    ]
    shard_loads = [
        pltpu.make_async_copy(kin_ref, w_in.at[:, in_slot(0)], l_sem.at[3]),
        pltpu.make_async_copy(kout_ref, w_out.at[in_slot(0)], l_sem.at[4]),
    ]
    for load in loads:
        load.start()

    @pl.when(core == 0)
    def _():
        for load in shard_loads:
            load.start()

    pl.semaphore_wait(barrier, len(peers))

    started = []
    started_on = ([], [])
    used = [0]

    def ids(count=1):
        used[0] += count
        return used[0] - count

    def copy_to(src, dst, k, device, k_recv=None):
        return pltpu.make_async_remote_copy(
            src_ref=src, dst_ref=dst, send_sem=s_sem.at[k], recv_sem=r_sem.at[k if k_recv is None else k_recv],
            device_id=device, device_id_type=MESH,
        )

    def send(src, dst, k, device, k_recv=None):
        copy = copy_to(src, dst, k, device, k_recv)
        copy.start()
        started.append(copy)

    def send_on(only, make):
        make().start()
        started_on[only].append(make)

    def arrive(dst, k):
        copy_to(dst, dst, k, mate).wait_recv()

    k_win, k_wout = ids(HALF + 1), ids(HALF + 1)
    k_mate_rows, k_x_rows, k_fwd_rows = ids(2), ids(2), ids(2)
    k_chain = ids(2 * HALF)
    k_fin, k_fin_anti, k_fin_mate = ids(4), ids(2), ids()
    k_back = ids(3)
    k_halo = ids(2)
    k_piece, k_tri, k_tot, k_swap = ids(npiece), ids(zg_n), ids(npiece), ids()
    assert used[0] <= N_SEM

    def w_at(m, slot):
        return w_in.at[:, in_slot(slot)] if m == 0 else w_out.at[in_slot(slot)]

    def arrive_shard(m, j):
        arrive(w_at(m, j - core), (k_win, k_wout)[m] + j)

    def forward_shard(m, j):
        send(w_at(m, j - core), w_at(m, j + 1 - core), (k_win, k_wout)[m] + j + 1, y_fwd)

    send(kin_ref, w_at(0, other), k_win + 1, y_fwd)
    send(kout_ref, w_at(1, other), k_wout + 1, y_fwd)
    send(agg_ref, rows_a.at[by_x], k_x_rows, across)
    send(cot_ref, rows_c.at[by_x], k_x_rows + 1, across)
    send(agg_ref, rows_a.at[by_mate], k_mate_rows, mate)
    send(cot_ref, rows_c.at[by_mate], k_mate_rows + 1, mate)

    def flip(block):
        at[:, block] = rows_a[block].T
        ct[:, block] = rows_c[block].T

    def unit(slot, rows):
        a, g = gelu_pair(dot(rows_a[rows], w_in[:, in_slot(slot)]), dot_last(rows_c[rows], w_out[in_slot(slot)]))
        act[rows, in_slot(slot)] = a
        gpre[rows, in_slot(slot)] = g

    def weight_term(slot, m):
        left, right = (at, gpre) if m == 0 else (ct, act)
        return dot(left[...], right[:, in_slot(slot)])

    for load in loads:
        load.wait()
    flip(own)
    arrive(rows_a.at[by_mate], k_mate_rows)
    arrive(rows_c.at[by_mate], k_mate_rows + 1)
    flip(by_mate)
    for m in range(2):
        arrive_shard(m, 1)
        forward_shard(m, 1)
    unit(1 - core, near)
    arrive(rows_a.at[by_x], k_x_rows)
    send(rows_a.at[by_x], rows_a.at[by_x_mate], k_fwd_rows, mate)
    for m in range(2):
        arrive_shard(m, 2)
        forward_shard(m, 2)
    arrive(rows_c.at[by_x], k_x_rows + 1)
    send(rows_c.at[by_x], rows_c.at[by_x_mate], k_fwd_rows + 1, mate)
    unit(2 - core, near)
    flip(by_x)
    arrive(rows_a.at[by_x_mate], k_fwd_rows)
    arrive(rows_c.at[by_x_mate], k_fwd_rows + 1)
    flip(by_x_mate)
    for m in range(2):
        arrive_shard(m, 3)

        @pl.when(core == 1)
        def _():
            send_on(1, lambda m=m: copy_to(w_at(m, 2), w_at(m, 3), (k_win, k_wout)[m] + HALF, y_fwd))

    unit(3 - core, every)
    for m in range(2):
        chain_out[3, m] = weight_term(3 - core, m).astype(BF16)
        send(chain_out.at[3, m], chain_in.at[3, m], k_chain + 6 + m, y_bwd)
    for j in (2, 1):
        unit(j - core, far)
        for m in range(2):
            part[j, m] = weight_term(j - core, m)

    @pl.when(core == 0)
    def _():
        for load in shard_loads:
            load.wait()

    @pl.when(core == 1)
    def _():
        for m in range(2):
            arrive(w_at(m, 3), (k_win, k_wout)[m] + HALF)

    unit(3 * core, every)
    for m in range(2):
        anti_out[m] = weight_term(3 * core, m).astype(BF16)

        @pl.when(core == 1)
        def _():
            send_on(1, lambda m=m: copy_to(anti_out.at[m], fin_in.at[2], k_fin_anti + m, along_y(HALF, m), k_fin_anti))

    @pl.when(core == 0)
    def _():
        send_on(0, lambda: copy_to(anti_out.at[1], fin_in.at[3], k_fin_mate, mate))
        fin_in[3] = anti_out[0]

    def shares(block):
        return dot_last(gpre[block], w_in[...])

    def chain_step(k, m):
        arrive(chain_in.at[k + 1, m], k_chain + 2 * (k + 1) + m)
        chain_out[k, m] = (part[k, m] + chain_in[k + 1, m].astype(F32)).astype(BF16)
        if k > 1:
            send(chain_out.at[k, m], chain_in.at[k, m], k_chain + 2 * k + m, y_bwd)
        else:
            send(chain_out.at[k, m], fin_in.at[core], k_fin + 2 * m, along_y(-sign, m), k_fin + core)

    for m in range(2):
        chain_step(2, m)
    back_out[1] = shares(by_x_mate).astype(BF16)
    send(back_out.at[1], back_in.at[1], k_back + 1, mate)
    back_out[0] = shares(by_mate).astype(BF16)
    send(back_out.at[0], back_in.at[0], k_back, mate)
    acc[...] = shares(by_x)
    arrive(back_in.at[1], k_back + 1)
    back_out[2] = (acc[...] + back_in[1].astype(F32)).astype(BF16)
    send(back_out.at[2], back_in.at[2], k_back + 2, across)
    for m in range(2):
        chain_step(1, m)
    acc[...] = shares(own)
    for t in range(tiles.shape[0]):
        tiles[t] = tiles[t].T

    @pl.when(core == 1)
    def _():
        arrive(fin_in.at[3], k_fin_mate)

    arrive(fin_in.at[2], k_fin_anti)
    mine = fin_in[3].astype(F32) + fin_in[2].astype(F32)
    for c in range(2):
        arrive(fin_in.at[c], k_fin + c)
        mine = mine + fin_in[c].astype(F32)

    prow = feat // npiece
    for p in range(npiece):
        pieces[p] = mine[p * prow : (p + 1) * prow].astype(BF16)
    for j, peer, p in scatter_peers:
        send(pieces.at[p], piece_in.at[j], k_piece + j, peer)

    arrive(back_in.at[0], k_back)
    arrive(back_in.at[2], k_back + 2)
    g_agg = (acc[...] + back_in[0].astype(F32) + back_in[2].astype(F32)).astype(BF16)
    live_count = count_ref[0]
    sums = [None, None, None]
    for t in range(tiles.shape[0]):
        term = dot(tiles[t], g_agg)
        for k in range(3):
            on = jnp.logical_and(cols_ref[0, t] == k, t < live_count)
            add = term * jnp.where(on, 1.0, 0.0).astype(F32)
            sums[k] = add if sums[k] is None else sums[k] + add
    halo_out[0] = sums[0].astype(BF16)
    halo_out[1] = sums[2].astype(BF16)
    acc[...] = sums[1] + rows_c[own].astype(F32)
    send(halo_out.at[0], halo_in.at[0], k_halo, prv)
    send(halo_out.at[1], halo_in.at[1], k_halo + 1, nxt)

    tot = pieces[my_piece].astype(F32)
    for j, peer, _ in scatter_peers:
        arrive(piece_in.at[j], k_piece + j)
        tot = tot + piece_in[j].astype(F32)
    triple[...] = tot.astype(BF16)
    for j, peer in tri_peers:
        send(triple, triple_in.at[zg], k_tri + j, peer)
    triple_in[zg] = triple[...]

    arrive(halo_in.at[0], k_halo)
    arrive(halo_in.at[1], k_halo + 1)
    nodes_buf[...] = (acc[...] + halo_in[1].astype(F32) + halo_in[0].astype(F32)).astype(BF16)
    out_nodes = pltpu.make_async_copy(nodes_buf, nodes_ref, l_sem.at[0])
    out_nodes.start()

    for j, peer in tri_peers:
        arrive(triple_in.at[lax.rem(zg + zg_n - j, zg_n)], k_tri + j)
    tot = triple_in[0].astype(F32)
    for k in range(1, zg_n):
        tot = tot + triple_in[k].astype(F32)
    total[core, my_piece] = tot.astype(BF16)
    for j, peer, _ in scatter_peers:
        send(total.at[core, my_piece], total.at[core, my_piece], k_tot + j, peer)
    for j, peer, _ in scatter_peers:
        fxh = lax.rem(xh + X_HI - j // Z_IN, X_HI)
        fzi = lax.rem(zi + Z_IN - j % Z_IN, Z_IN)
        arrive(total.at[core, fxh * Z_IN + fzi], k_tot + j)
    send(total.at[core], total.at[core], k_swap, mate)
    arrive(total.at[other], k_swap)
    for p in range(npiece):
        gin_buf[p * prow : (p + 1) * prow, :] = total[0, p].astype(F32) * norm_factor
    out_gin = pltpu.make_async_copy(gin_buf, gin_ref, l_sem.at[1])
    out_gin.start()
    gout_buf[...] = jnp.concatenate([total[1, p] for p in range(npiece)], axis=0).T.astype(F32) * norm_factor
    out_gout = pltpu.make_async_copy(gout_buf, gout_ref, l_sem.at[2])
    out_gout.start()
    for copy in started:
        copy.wait_send()
    for only in range(2):

        @pl.when(core == only)
        def _():
            for make in started_on[only]:
                make().wait_send()

    out_nodes.wait()
    out_gin.wait()
    out_gout.wait()


def hand_over(*refs):
    n = len(refs) // 3
    sems = refs[-1]
    fetch = [pltpu.make_async_copy(refs[k], refs[2 * n + k], sems.at[k]) for k in range(n)]
    store = [pltpu.make_async_copy(refs[2 * n + k], refs[n + k], sems.at[n + k]) for k in range(n)]
    for copy in fetch:
        copy.start()
    for k in range(n):
        fetch[k].wait()
        store[k].start()
    for copy in store:
        copy.wait()


def local(nz, aggregated, cotangent, kernel_in, kernel_out, tile_values, tile_cols, tile_count):
    nrow, feat = aggregated.shape
    assert lax.axis_size("rep") == NY * X_LO
    hid = kernel_in.shape[1]
    slots = tile_values.shape[1]
    npiece = X_HI * Z_IN
    zg_n = nz // Z_IN
    prow = feat // npiece
    norm_factor = 1.0 / math.sqrt(nrow * lax.axis_size("node") * lax.axis_size("rep"))
    vmem = lambda shape, dtype=BF16: pltpu.VMEM(shape, dtype)
    hbm = pl.BlockSpec(memory_space=pltpu.HBM)
    scalars = pl.BlockSpec(memory_space=pltpu.SMEM)
    shapes = (
        jax.ShapeDtypeStruct((nrow, feat), BF16),
        jax.ShapeDtypeStruct((feat, hid), F32),
        jax.ShapeDtypeStruct((hid, feat), F32),
    )
    results = pl.pallas_call(
        functools.partial(kernel, nz, norm_factor),
        out_shape=shapes,
        in_specs=[hbm] * 5 + [scalars] * 2,
        out_specs=(hbm, hbm, hbm),
        scratch_shapes=[
            vmem((4 * nrow, feat)),
            vmem((4 * nrow, feat)),
            vmem((feat, 4 * nrow)),
            vmem((feat, 4 * nrow)),
            vmem((slots, nrow, nrow)),
            vmem((feat, HALF * hid)),
            vmem((HALF * hid, feat)),
            vmem((4 * nrow, HALF * hid)),
            vmem((4 * nrow, HALF * hid)),
            vmem((HALF, 2, feat, hid), F32),
            vmem((HALF, 2, feat, hid)),
            vmem((HALF, 2, feat, hid)),
            vmem((2, feat, hid)),
            vmem((4, feat, hid)),
            vmem((nrow, feat), F32),
            vmem((3, nrow, feat)),
            vmem((3, nrow, feat)),
            vmem((2, nrow, feat)),
            vmem((2, nrow, feat)),
            vmem((npiece, prow, hid)),
            vmem((npiece, prow, hid)),
            vmem((prow, hid)),
            vmem((zg_n, prow, hid)),
            vmem((2, npiece, prow, hid)),
            vmem((nrow, feat)),
            vmem((feat, hid), F32),
            vmem((hid, feat), F32),
            pltpu.SemaphoreType.DMA((N_SEM,)),
            pltpu.SemaphoreType.DMA((N_SEM,)),
            pltpu.SemaphoreType.DMA((5,)),
        ],
        compiler_params=pltpu.CompilerParams(
            collective_id=0, has_side_effects=True, vmem_limit_bytes=62 << 20
        ),
    )(aggregated, cotangent, kernel_in, kernel_out, tile_values, tile_cols, tile_count)
    return pl.pallas_call(
        hand_over,
        out_shape=shapes,
        in_specs=[hbm] * 3,
        out_specs=(hbm, hbm, hbm),
        scratch_shapes=[vmem(s.shape, s.dtype) for s in shapes] + [pltpu.SemaphoreType.DMA((6,))],
        compiler_params=pltpu.CompilerParams(vmem_limit_bytes=62 << 20),
    )(*results)


def solution(mesh):
    nz = mesh.shape["node"] // (X_HI * CORES)
    return jax.shard_map(
        functools.partial(local, nz),
        mesh=mesh,
        in_specs=(
            P(("node", "rep"), None),
            P(("node", "rep"), None),
            P(None, "rep"),
            P("rep", None),
            P(("node", "rep"), None, None, None),
            P(("node", "rep"), None),
            P(("node", "rep")),
        ),
        out_specs=(P(("node", "rep"), None), P(None, "rep"), P("rep", None)),
        check_vma=False,
    )
```

```python
import functools
import math

import jax
import jax.numpy as jnp
from jax import lax
from jax.experimental import pallas as pl
from jax.experimental.pallas import tpu as pltpu
from jax.sharding import PartitionSpec as P

MESH = pl.DeviceIdType.MESH
BF16 = jnp.bfloat16
F32 = jnp.float32
X_HI, X_LO, CORES, NY, Z_IN = 2, 2, 2, 8, 4
HALF = NY // 2
GELU_C = math.sqrt(2.0 / math.pi)
N_SEM = 96
CUTS = 2


def dot(left, right):
    return jnp.dot(left, right, preferred_element_type=F32)


def dot_last(left, right):
    return lax.dot_general(left, right, (((1,), (1,)), ((), ())), preferred_element_type=F32)


def gelu_pair(pre, g_act):
    sq = pre * pre
    th = jnp.tanh(GELU_C * (pre + 0.044715 * sq * pre))
    half = 0.5 * (1.0 + th)
    slope = half + 0.5 * pre * (1.0 - th * th) * GELU_C * (1.0 + 3.0 * 0.044715 * sq)
    return (pre * half).astype(BF16), (g_act * slope).astype(BF16)


def kernel(
    nz, norm_factor,
    agg_ref, cot_ref, kin_ref, kout_ref, tiles_ref, cols_ref, count_ref,
    nodes_ref, gin_ref, gout_ref,
    rows_a, rows_c, at, ct, tiles, w_in, w_out, act, gpre, part, chain_out, chain_in, anti_out, fin_in,
    acc, back_out, back_in, halo_out, halo_in, pieces, piece_in, triple, triple_in, total,
    nodes_buf, gin_buf, gout_buf,
    s_sem, r_sem, l_sem,
):
    zg_n = nz // Z_IN
    npiece = X_HI * Z_IN
    nrow, feat = agg_ref.shape
    hid = kin_ref.shape[1]
    node, rep = lax.axis_index("node"), lax.axis_index("rep")
    core = lax.rem(node, CORES)
    z = lax.rem(lax.div(node, CORES), nz)
    xh = lax.div(node, CORES * nz)
    y, xl = lax.div(rep, X_LO), lax.rem(rep, X_LO)
    zg, zi = lax.div(z, Z_IN), lax.rem(z, Z_IN)
    other = 1 - core
    sign = 1 - 2 * core
    nodes = X_HI * nz * CORES

    def dev(xh, xl, y, z, core):
        return (xh * (nz * CORES) + z * CORES + core, y * X_LO + xl)

    def along_y(step, on_core):
        return dev(xh, xl, lax.rem(y + step + NY, NY), z, on_core)

    mate = dev(xh, xl, y, z, other)
    across = dev(lax.rem(xh + core, X_HI), 1 - xl, y, z, core)
    y_fwd, y_bwd = along_y(sign, core), along_y(-sign, core)
    nxt = (lax.rem(node + 1, nodes), rep)
    prv = (lax.rem(node + nodes - 1, nodes), rep)
    my_piece = xh * Z_IN + zi
    scatter_peers = []
    for j in range(1, npiece):
        pxh = lax.rem(xh + j // Z_IN, X_HI)
        pzi = lax.rem(zi + j % Z_IN, Z_IN)
        scatter_peers.append((j, dev(pxh, xl, y, zg * Z_IN + pzi, core), pxh * Z_IN + pzi))
    tri_peers = []
    for j in range(1, zg_n):
        tri_peers.append((j, dev(xh, xl, y, lax.rem(zg + j, zg_n) * Z_IN + zi, core)))

    barrier = pltpu.get_barrier_semaphore()
    peers = [y_fwd, y_bwd, across, mate, along_y(sign, other), along_y(-sign, other)]
    peers += [along_y(HALF, core), along_y(HALF, other), nxt, prv]
    peers += [d for _, d, _ in scatter_peers] + [d for _, d in tri_peers]
    for peer in peers:
        pl.semaphore_signal(barrier, inc=1, device_id=peer, device_id_type=MESH)

    def in_slot(slot):
        start = slot * hid
        return pl.ds(start if isinstance(slot, int) else pl.multiple_of(start, hid), hid)

    own, by_mate, by_x, by_x_mate = [pl.ds(k * nrow, nrow) for k in range(4)]
    near, far = pl.ds(0, 2 * nrow), pl.ds(2 * nrow, 2 * nrow)
    every = pl.ds(0, 4 * nrow)
    loads = [
        pltpu.make_async_copy(agg_ref, rows_a.at[own], l_sem.at[0]),
        pltpu.make_async_copy(cot_ref, rows_c.at[own], l_sem.at[1]),
        pltpu.make_async_copy(tiles_ref.at[0], tiles, l_sem.at[2]),
    ]
    shard_loads = [
        pltpu.make_async_copy(kin_ref, w_in.at[:, in_slot(0)], l_sem.at[3]),
        pltpu.make_async_copy(kout_ref, w_out.at[in_slot(0)], l_sem.at[4]),
    ]
    for load in loads:
        load.start()

    @pl.when(core == 0)
    def _():
        for load in shard_loads:
            load.start()

    pl.semaphore_wait(barrier, len(peers))

    started = []
    started_on = ([], [])
    used = [0]

    def ids(count=1):
        used[0] += count
        return used[0] - count

    def copy_to(src, dst, k, device, k_recv=None):
        return pltpu.make_async_remote_copy(
            src_ref=src, dst_ref=dst, send_sem=s_sem.at[k], recv_sem=r_sem.at[k if k_recv is None else k_recv],
            device_id=device, device_id_type=MESH,
        )

    def send(src, dst, k, device, k_recv=None):
        copy = copy_to(src, dst, k, device, k_recv)
        copy.start()
        started.append(copy)

    def send_on(only, make):
        make().start()
        started_on[only].append(make)

    def arrive(dst, k):
        copy_to(dst, dst, k, mate).wait_recv()

    k_shard = [ids((HALF + 1) * CUTS) for _ in range(2)]
    k_mate_rows, k_x_rows, k_fwd_rows = ids(2), ids(2), ids(2)
    k_chain = ids(HALF * 2 * CUTS)
    k_fin, k_fin_anti, k_fin_mate = ids(4 * CUTS), ids(2), ids()
    k_back = ids(3)
    k_halo = ids(2)
    k_piece, k_tri, k_tot, k_swap = ids(npiece), ids(zg_n), ids(npiece), ids()
    assert used[0] <= N_SEM

    def w_at(m, slot, h):
        if m == 0:
            return w_in.at[pl.ds(h * (feat // CUTS), feat // CUTS), in_slot(slot)]
        size = hid // CUTS
        start = slot * hid + h * size
        return w_out.at[pl.ds(start if isinstance(slot, int) else pl.multiple_of(start, size), size)]

    pieces_of = [(m, h) for m in range(2) for h in range(CUTS)]

    def arrive_shard(m, h, j, slot):
        arrive(w_at(m, slot, h), k_shard[m] + j * CUTS + h)

    def forward_shard(m, h, j):
        send(w_at(m, j - core, h), w_at(m, j + 1 - core, h), k_shard[m] + (j + 1) * CUTS + h, y_fwd)

    for m, h in pieces_of:
        shard = (kin_ref, kout_ref)[m]
        size = shard.shape[0] // CUTS
        send(shard.at[pl.ds(h * size, size)], w_at(m, other, h), k_shard[m] + CUTS + h, y_fwd)
    send(agg_ref, rows_a.at[by_x], k_x_rows, across)
    send(cot_ref, rows_c.at[by_x], k_x_rows + 1, across)
    send(agg_ref, rows_a.at[by_mate], k_mate_rows, mate)
    send(cot_ref, rows_c.at[by_mate], k_mate_rows + 1, mate)

    def flip(block):
        at[:, block] = rows_a[block].T
        ct[:, block] = rows_c[block].T

    def unit(slot, rows):
        a, g = gelu_pair(dot(rows_a[rows], w_in[:, in_slot(slot)]), dot_last(rows_c[rows], w_out[in_slot(slot)]))
        act[rows, in_slot(slot)] = a
        gpre[rows, in_slot(slot)] = g

    def weight_term(slot, m):
        left, right = (at, gpre) if m == 0 else (ct, act)
        return dot(left[...], right[:, in_slot(slot)])

    for load in loads:
        load.wait()
    flip(own)
    arrive(rows_a.at[by_mate], k_mate_rows)
    arrive(rows_c.at[by_mate], k_mate_rows + 1)
    flip(by_mate)
    for m, h in pieces_of:
        arrive_shard(m, h, 1, 1 - core)
        forward_shard(m, h, 1)
    unit(1 - core, near)
    arrive(rows_a.at[by_x], k_x_rows)
    send(rows_a.at[by_x], rows_a.at[by_x_mate], k_fwd_rows, mate)
    for m, h in pieces_of:
        arrive_shard(m, h, 2, 2 - core)
        forward_shard(m, h, 2)
    arrive(rows_c.at[by_x], k_x_rows + 1)
    send(rows_c.at[by_x], rows_c.at[by_x_mate], k_fwd_rows + 1, mate)
    unit(2 - core, near)
    flip(by_x)
    arrive(rows_a.at[by_x_mate], k_fwd_rows)
    arrive(rows_c.at[by_x_mate], k_fwd_rows + 1)
    flip(by_x_mate)
    for m, h in pieces_of:
        arrive_shard(m, h, 3, 3 - core)

        @pl.when(core == 1)
        def _():
            send_on(1, lambda m=m, h=h: copy_to(w_at(m, 2, h), w_at(m, 3, h), k_shard[m] + HALF * CUTS + h, y_fwd))

    def rows_of(h):
        return pl.ds(h * (feat // CUTS), feat // CUTS)

    def k_link(k, m, h):
        return k_chain + (k * 2 + m) * CUTS + h

    unit(3 - core, every)
    for m in range(2):
        chain_out[3, m] = weight_term(3 - core, m).astype(BF16)
        for h in range(CUTS):
            send(chain_out.at[3, m, rows_of(h)], chain_in.at[3, m, rows_of(h)], k_link(3, m, h), y_bwd)
    for j in (2, 1):
        unit(j - core, far)
        for m in range(2):
            part[j, m] = weight_term(j - core, m)

    @pl.when(core == 0)
    def _():
        for load in shard_loads:
            load.wait()

    @pl.when(core == 1)
    def _():
        for m, h in pieces_of:
            arrive_shard(m, h, HALF, 3)

    unit(3 * core, every)
    for m in range(2):
        anti_out[m] = weight_term(3 * core, m).astype(BF16)

        @pl.when(core == 1)
        def _():
            send_on(1, lambda m=m: copy_to(anti_out.at[m], fin_in.at[2], k_fin_anti + m, along_y(HALF, m), k_fin_anti))

    @pl.when(core == 0)
    def _():
        send_on(0, lambda: copy_to(anti_out.at[1], fin_in.at[3], k_fin_mate, mate))
        fin_in[3] = anti_out[0]

    def shares(block):
        return dot_last(gpre[block], w_in[...])

    def chain_step(k, m, h):
        cut = rows_of(h)
        arrive(chain_in.at[k + 1, m, cut], k_link(k + 1, m, h))
        chain_out[k, m, cut] = (part[k, m, cut] + chain_in[k + 1, m, cut].astype(F32)).astype(BF16)
        if k > 1:
            send(chain_out.at[k, m, cut], chain_in.at[k, m, cut], k_link(k, m, h), y_bwd)
        else:
            to = along_y(-sign, m)
            send(chain_out.at[k, m, cut], fin_in.at[core, cut], k_fin + (2 + m) * CUTS + h, to, k_fin + core * CUTS + h)

    for m, h in pieces_of:
        chain_step(2, m, h)
    back_out[1] = shares(by_x_mate).astype(BF16)
    send(back_out.at[1], back_in.at[1], k_back + 1, mate)
    back_out[0] = shares(by_mate).astype(BF16)
    send(back_out.at[0], back_in.at[0], k_back, mate)
    acc[...] = shares(by_x)
    arrive(back_in.at[1], k_back + 1)
    back_out[2] = (acc[...] + back_in[1].astype(F32)).astype(BF16)
    send(back_out.at[2], back_in.at[2], k_back + 2, across)
    for m, h in pieces_of:
        chain_step(1, m, h)
    acc[...] = shares(own)
    for t in range(tiles.shape[0]):
        tiles[t] = tiles[t].T

    @pl.when(core == 1)
    def _():
        arrive(fin_in.at[3], k_fin_mate)

    arrive(fin_in.at[2], k_fin_anti)
    mine = fin_in[3].astype(F32) + fin_in[2].astype(F32)
    for c in range(2):
        for h in range(CUTS):
            arrive(fin_in.at[c, rows_of(h)], k_fin + c * CUTS + h)
        mine = mine + fin_in[c].astype(F32)

    prow = feat // npiece
    for p in range(npiece):
        pieces[p] = mine[p * prow : (p + 1) * prow].astype(BF16)
    for j, peer, p in scatter_peers:
        send(pieces.at[p], piece_in.at[j], k_piece + j, peer)

    arrive(back_in.at[0], k_back)
    arrive(back_in.at[2], k_back + 2)
    g_agg = (acc[...] + back_in[0].astype(F32) + back_in[2].astype(F32)).astype(BF16)
    live_count = count_ref[0]
    sums = [None, None, None]
    for t in range(tiles.shape[0]):
        term = dot(tiles[t], g_agg)
        for k in range(3):
            on = jnp.logical_and(cols_ref[0, t] == k, t < live_count)
            add = term * jnp.where(on, 1.0, 0.0).astype(F32)
            sums[k] = add if sums[k] is None else sums[k] + add
    halo_out[0] = sums[0].astype(BF16)
    halo_out[1] = sums[2].astype(BF16)
    acc[...] = sums[1] + rows_c[own].astype(F32)
    send(halo_out.at[0], halo_in.at[0], k_halo, prv)
    send(halo_out.at[1], halo_in.at[1], k_halo + 1, nxt)

    tot = pieces[my_piece].astype(F32)
    for j, peer, _ in scatter_peers:
        arrive(piece_in.at[j], k_piece + j)
        tot = tot + piece_in[j].astype(F32)
    triple[...] = tot.astype(BF16)
    for j, peer in tri_peers:
        send(triple, triple_in.at[zg], k_tri + j, peer)
    triple_in[zg] = triple[...]

    arrive(halo_in.at[0], k_halo)
    arrive(halo_in.at[1], k_halo + 1)
    nodes_buf[...] = (acc[...] + halo_in[1].astype(F32) + halo_in[0].astype(F32)).astype(BF16)
    out_nodes = pltpu.make_async_copy(nodes_buf, nodes_ref, l_sem.at[0])
    out_nodes.start()

    for j, peer in tri_peers:
        arrive(triple_in.at[lax.rem(zg + zg_n - j, zg_n)], k_tri + j)
    tot = triple_in[0].astype(F32)
    for k in range(1, zg_n):
        tot = tot + triple_in[k].astype(F32)
    total[core, my_piece] = tot.astype(BF16)
    for j, peer, _ in scatter_peers:
        send(total.at[core, my_piece], total.at[core, my_piece], k_tot + j, peer)
    for j, peer, _ in scatter_peers:
        fxh = lax.rem(xh + X_HI - j // Z_IN, X_HI)
        fzi = lax.rem(zi + Z_IN - j % Z_IN, Z_IN)
        arrive(total.at[core, fxh * Z_IN + fzi], k_tot + j)
    send(total.at[core], total.at[core], k_swap, mate)
    arrive(total.at[other], k_swap)
    for p in range(npiece):
        gin_buf[p * prow : (p + 1) * prow, :] = total[0, p].astype(F32) * norm_factor
    out_gin = pltpu.make_async_copy(gin_buf, gin_ref, l_sem.at[1])
    out_gin.start()
    gout_buf[...] = jnp.concatenate([total[1, p] for p in range(npiece)], axis=0).T.astype(F32) * norm_factor
    out_gout = pltpu.make_async_copy(gout_buf, gout_ref, l_sem.at[2])
    out_gout.start()
    for copy in started:
        copy.wait_send()
    for only in range(2):

        @pl.when(core == only)
        def _():
            for make in started_on[only]:
                make().wait_send()

    out_nodes.wait()
    out_gin.wait()
    out_gout.wait()


def hand_over(*refs):
    n = len(refs) // 3
    sems = refs[-1]
    fetch = [pltpu.make_async_copy(refs[k], refs[2 * n + k], sems.at[k]) for k in range(n)]
    store = [pltpu.make_async_copy(refs[2 * n + k], refs[n + k], sems.at[n + k]) for k in range(n)]
    for copy in fetch:
        copy.start()
    for k in range(n):
        fetch[k].wait()
        store[k].start()
    for copy in store:
        copy.wait()


def local(nz, aggregated, cotangent, kernel_in, kernel_out, tile_values, tile_cols, tile_count):
    nrow, feat = aggregated.shape
    assert lax.axis_size("rep") == NY * X_LO
    hid = kernel_in.shape[1]
    slots = tile_values.shape[1]
    npiece = X_HI * Z_IN
    zg_n = nz // Z_IN
    prow = feat // npiece
    norm_factor = 1.0 / math.sqrt(nrow * lax.axis_size("node") * lax.axis_size("rep"))
    vmem = lambda shape, dtype=BF16: pltpu.VMEM(shape, dtype)
    hbm = pl.BlockSpec(memory_space=pltpu.HBM)
    scalars = pl.BlockSpec(memory_space=pltpu.SMEM)
    shapes = (
        jax.ShapeDtypeStruct((nrow, feat), BF16),
        jax.ShapeDtypeStruct((feat, hid), F32),
        jax.ShapeDtypeStruct((hid, feat), F32),
    )
    results = pl.pallas_call(
        functools.partial(kernel, nz, norm_factor),
        out_shape=shapes,
        in_specs=[hbm] * 5 + [scalars] * 2,
        out_specs=(hbm, hbm, hbm),
        scratch_shapes=[
            vmem((4 * nrow, feat)),
            vmem((4 * nrow, feat)),
            vmem((feat, 4 * nrow)),
            vmem((feat, 4 * nrow)),
            vmem((slots, nrow, nrow)),
            vmem((feat, HALF * hid)),
            vmem((HALF * hid, feat)),
            vmem((4 * nrow, HALF * hid)),
            vmem((4 * nrow, HALF * hid)),
            vmem((HALF, 2, feat, hid), F32),
            vmem((HALF, 2, feat, hid)),
            vmem((HALF, 2, feat, hid)),
            vmem((2, feat, hid)),
            vmem((4, feat, hid)),
            vmem((nrow, feat), F32),
            vmem((3, nrow, feat)),
            vmem((3, nrow, feat)),
            vmem((2, nrow, feat)),
            vmem((2, nrow, feat)),
            vmem((npiece, prow, hid)),
            vmem((npiece, prow, hid)),
            vmem((prow, hid)),
            vmem((zg_n, prow, hid)),
            vmem((2, npiece, prow, hid)),
            vmem((nrow, feat)),
            vmem((feat, hid), F32),
            vmem((hid, feat), F32),
            pltpu.SemaphoreType.DMA((N_SEM,)),
            pltpu.SemaphoreType.DMA((N_SEM,)),
            pltpu.SemaphoreType.DMA((5,)),
        ],
        compiler_params=pltpu.CompilerParams(
            collective_id=0, has_side_effects=True, vmem_limit_bytes=62 << 20
        ),
    )(aggregated, cotangent, kernel_in, kernel_out, tile_values, tile_cols, tile_count)
    return pl.pallas_call(
        hand_over,
        out_shape=shapes,
        in_specs=[hbm] * 3,
        out_specs=(hbm, hbm, hbm),
        scratch_shapes=[vmem(s.shape, s.dtype) for s in shapes] + [pltpu.SemaphoreType.DMA((6,))],
        compiler_params=pltpu.CompilerParams(vmem_limit_bytes=62 << 20),
    )(*results)


def solution(mesh):
    nz = mesh.shape["node"] // (X_HI * CORES)
    return jax.shard_map(
        functools.partial(local, nz),
        mesh=mesh,
        in_specs=(
            P(("node", "rep"), None),
            P(("node", "rep"), None),
            P(None, "rep"),
            P("rep", None),
            P(("node", "rep"), None, None, None),
            P(("node", "rep"), None),
            P(("node", "rep")),
        ),
        out_specs=(P(("node", "rep"), None), P(None, "rep"), P("rep", None)),
        check_vma=False,
    )
```

```python
import functools
import math

import jax
import jax.numpy as jnp
from jax import lax
from jax.experimental import pallas as pl
from jax.experimental.pallas import tpu as pltpu
from jax.sharding import PartitionSpec as P

MESH = pl.DeviceIdType.MESH
BF16 = jnp.bfloat16
F32 = jnp.float32
X_HI, X_LO, CORES, NY, Z_IN = 2, 2, 2, 8, 4
HALF = NY // 2
GELU_C = math.sqrt(2.0 / math.pi)
N_SEM = 96
CUTS = 2


def dot(left, right):
    return jnp.dot(left, right, preferred_element_type=F32)


def dot_last(left, right):
    return lax.dot_general(left, right, (((1,), (1,)), ((), ())), preferred_element_type=F32)


def gelu_pair(pre, g_act):
    sq = pre * pre
    th = jnp.tanh(GELU_C * (pre + 0.044715 * sq * pre))
    half = 0.5 * (1.0 + th)
    slope = half + 0.5 * pre * (1.0 - th * th) * GELU_C * (1.0 + 3.0 * 0.044715 * sq)
    return (pre * half).astype(BF16), (g_act * slope).astype(BF16)


def kernel(
    nz, norm_factor,
    agg_ref, cot_ref, kin_ref, kout_ref, tiles_ref, cols_ref, count_ref,
    nodes_ref, gin_ref, gout_ref,
    rows_a, rows_c, at, ct, tiles, w_in, w_out, act, gpre, part, chain_out, chain_in, anti_out, fin_in,
    shares, sums, g_agg, back_out, back_in, halo_out, halo_in, pieces, piece_in, triple, triple_in, total,
    nodes_buf, gin_buf, gout_buf,
    s_sem, r_sem, l_sem,
):
    zg_n = nz // Z_IN
    npiece = X_HI * Z_IN
    nrow, feat = agg_ref.shape
    hid = kin_ref.shape[1]
    node, rep = lax.axis_index("node"), lax.axis_index("rep")
    core = lax.rem(node, CORES)
    z = lax.rem(lax.div(node, CORES), nz)
    xh = lax.div(node, CORES * nz)
    y, xl = lax.div(rep, X_LO), lax.rem(rep, X_LO)
    zg, zi = lax.div(z, Z_IN), lax.rem(z, Z_IN)
    other = 1 - core
    sign = 1 - 2 * core
    nodes = X_HI * nz * CORES

    def dev(xh, xl, y, z, core):
        return (xh * (nz * CORES) + z * CORES + core, y * X_LO + xl)

    def along_y(step, on_core):
        return dev(xh, xl, lax.rem(y + step + NY, NY), z, on_core)

    mate = dev(xh, xl, y, z, other)
    across = dev(lax.rem(xh + core, X_HI), 1 - xl, y, z, core)
    y_fwd, y_bwd = along_y(sign, core), along_y(-sign, core)
    nxt = (lax.rem(node + 1, nodes), rep)
    prv = (lax.rem(node + nodes - 1, nodes), rep)
    my_piece = xh * Z_IN + zi
    scatter_peers = []
    for j in range(1, npiece):
        pxh = lax.rem(xh + j // Z_IN, X_HI)
        pzi = lax.rem(zi + j % Z_IN, Z_IN)
        scatter_peers.append((j, dev(pxh, xl, y, zg * Z_IN + pzi, core), pxh * Z_IN + pzi))
    tri_peers = []
    for j in range(1, zg_n):
        tri_peers.append((j, dev(xh, xl, y, lax.rem(zg + j, zg_n) * Z_IN + zi, core)))

    barrier = pltpu.get_barrier_semaphore()
    peers = [y_fwd, y_bwd, across, mate, along_y(sign, other), along_y(-sign, other)]
    peers += [along_y(HALF, core), along_y(HALF, other), nxt, prv]
    peers += [d for _, d, _ in scatter_peers] + [d for _, d in tri_peers]
    for peer in peers:
        pl.semaphore_signal(barrier, inc=1, device_id=peer, device_id_type=MESH)

    def in_slot(slot):
        start = slot * hid
        return pl.ds(start if isinstance(slot, int) else pl.multiple_of(start, hid), hid)

    own, by_mate, by_x, by_x_mate = [pl.ds(k * nrow, nrow) for k in range(4)]
    loads = [
        pltpu.make_async_copy(agg_ref, rows_a.at[own], l_sem.at[0]),
        pltpu.make_async_copy(cot_ref, rows_c.at[own], l_sem.at[1]),
        pltpu.make_async_copy(tiles_ref.at[0], tiles, l_sem.at[2]),
    ]
    shard_loads = [
        pltpu.make_async_copy(kin_ref, w_in.at[:, in_slot(0)], l_sem.at[3]),
        pltpu.make_async_copy(kout_ref, w_out.at[in_slot(0)], l_sem.at[4]),
    ]
    for load in loads:
        load.start()

    @pl.when(core == 0)
    def _():
        for load in shard_loads:
            load.start()

    pl.semaphore_wait(barrier, len(peers))

    started = []
    started_on = ([], [])
    used = [0]

    def ids(count=1):
        used[0] += count
        return used[0] - count

    def copy_to(src, dst, k, device, k_recv=None):
        return pltpu.make_async_remote_copy(
            src_ref=src, dst_ref=dst, send_sem=s_sem.at[k], recv_sem=r_sem.at[k if k_recv is None else k_recv],
            device_id=device, device_id_type=MESH,
        )

    def send(src, dst, k, device, k_recv=None):
        copy = copy_to(src, dst, k, device, k_recv)
        copy.start()
        started.append(copy)

    def send_on(only, make):
        make().start()
        started_on[only].append(make)

    def arrive(dst, k):
        copy_to(dst, dst, k, mate).wait_recv()

    k_shard = [ids((HALF + 1) * CUTS) for _ in range(2)]
    k_mate_rows, k_x_rows, k_fwd_rows = ids(2), ids(2), ids(2)
    k_chain = ids(HALF * 2 * CUTS)
    k_fin, k_fin_anti, k_fin_mate = ids(4 * CUTS), ids(2), ids()
    k_back = ids(3)
    k_halo = ids(2)
    k_piece, k_tri, k_tot, k_swap = ids(npiece), ids(zg_n), ids(npiece), ids()
    assert used[0] <= N_SEM

    def w_at(m, slot, h):
        if m == 0:
            return w_in.at[pl.ds(h * (feat // CUTS), feat // CUTS), in_slot(slot)]
        size = hid // CUTS
        start = slot * hid + h * size
        return w_out.at[pl.ds(start if isinstance(slot, int) else pl.multiple_of(start, size), size)]

    pieces_of = [(m, h) for m in range(2) for h in range(CUTS)]

    def arrive_shard(m, h, j, slot):
        arrive(w_at(m, slot, h), k_shard[m] + j * CUTS + h)

    def forward_shard(m, h, j):
        send(w_at(m, j - core, h), w_at(m, j + 1 - core, h), k_shard[m] + (j + 1) * CUTS + h, y_fwd)

    for m, h in pieces_of:
        shard = (kin_ref, kout_ref)[m]
        size = shard.shape[0] // CUTS
        send(shard.at[pl.ds(h * size, size)], w_at(m, other, h), k_shard[m] + CUTS + h, y_fwd)
    send(agg_ref, rows_a.at[by_x], k_x_rows, across)
    send(cot_ref, rows_c.at[by_x], k_x_rows + 1, across)
    send(agg_ref, rows_a.at[by_mate], k_mate_rows, mate)
    send(cot_ref, rows_c.at[by_mate], k_mate_rows + 1, mate)

    def chunks(count, size, body):
        def step(i, carry):
            body(pl.ds(pl.multiple_of(i * size, size), size))
            return carry

        lax.fori_loop(0, count, step, 0)

    def flip(block):
        def body(cols):
            at[cols, block] = rows_a[block, cols].T
            ct[cols, block] = rows_c[block, cols].T

        chunks(feat // hid, hid, body)

    def unit(slot, first, count):
        cols = in_slot(slot)

        def step(i, carry):
            rows = pl.ds(pl.multiple_of(i * nrow, nrow), nrow)
            a, g = gelu_pair(dot(rows_a[rows], w_in[:, cols]), dot_last(rows_c[rows], w_out[cols]))
            act[rows, cols] = a
            gpre[rows, cols] = g
            return carry

        lax.fori_loop(first, first + count, step, 0)

    def weight_term(slot, m, dst):
        left, right = (at, gpre) if m == 0 else (ct, act)
        cols = in_slot(slot)

        def body(rows):
            dst[rows] = dot(left[rows], right[:, cols]).astype(dst.dtype)

        chunks(2, feat // 2, body)

    for load in loads:
        load.wait()
    flip(own)
    arrive(rows_a.at[by_mate], k_mate_rows)
    arrive(rows_c.at[by_mate], k_mate_rows + 1)
    flip(by_mate)
    for m, h in pieces_of:
        arrive_shard(m, h, 1, 1 - core)
        forward_shard(m, h, 1)
    unit(1 - core, 0, 2)
    arrive(rows_a.at[by_x], k_x_rows)
    send(rows_a.at[by_x], rows_a.at[by_x_mate], k_fwd_rows, mate)
    for m, h in pieces_of:
        arrive_shard(m, h, 2, 2 - core)
        forward_shard(m, h, 2)
    arrive(rows_c.at[by_x], k_x_rows + 1)
    send(rows_c.at[by_x], rows_c.at[by_x_mate], k_fwd_rows + 1, mate)
    unit(2 - core, 0, 2)
    flip(by_x)
    arrive(rows_a.at[by_x_mate], k_fwd_rows)
    arrive(rows_c.at[by_x_mate], k_fwd_rows + 1)
    flip(by_x_mate)
    for m, h in pieces_of:
        arrive_shard(m, h, 3, 3 - core)

        @pl.when(core == 1)
        def _():
            send_on(1, lambda m=m, h=h: copy_to(w_at(m, 2, h), w_at(m, 3, h), k_shard[m] + HALF * CUTS + h, y_fwd))

    def rows_of(h):
        return pl.ds(h * (feat // CUTS), feat // CUTS)

    def k_link(k, m, h):
        return k_chain + (k * 2 + m) * CUTS + h

    unit(3 - core, 0, 4)
    for m in range(2):
        weight_term(3 - core, m, chain_out.at[3, m])
        for h in range(CUTS):
            send(chain_out.at[3, m, rows_of(h)], chain_in.at[3, m, rows_of(h)], k_link(3, m, h), y_bwd)
    for j in (2, 1):
        unit(j - core, 2, 2)
        for m in range(2):
            weight_term(j - core, m, part.at[j, m])

    @pl.when(core == 0)
    def _():
        for load in shard_loads:
            load.wait()

    @pl.when(core == 1)
    def _():
        for m, h in pieces_of:
            arrive_shard(m, h, HALF, 3)

    unit(3 * core, 0, 4)
    for m in range(2):
        weight_term(3 * core, m, anti_out.at[m])

        @pl.when(core == 1)
        def _():
            send_on(1, lambda m=m: copy_to(anti_out.at[m], fin_in.at[2], k_fin_anti + m, along_y(HALF, m), k_fin_anti))

    @pl.when(core == 0)
    def _():
        send_on(0, lambda: copy_to(anti_out.at[1], fin_in.at[3], k_fin_mate, mate))
        fin_in[3] = anti_out[0]

    def chain_step(k, m, h):
        cut = rows_of(h)
        arrive(chain_in.at[k + 1, m, cut], k_link(k + 1, m, h))
        chain_out[k, m, cut] = (part[k, m, cut] + chain_in[k + 1, m, cut].astype(F32)).astype(BF16)
        if k > 1:
            send(chain_out.at[k, m, cut], chain_in.at[k, m, cut], k_link(k, m, h), y_bwd)
        else:
            to = along_y(-sign, m)
            send(chain_out.at[k, m, cut], fin_in.at[core, cut], k_fin + (2 + m) * CUTS + h, to, k_fin + core * CUTS + h)

    for m, h in pieces_of:
        chain_step(2, m, h)
    def share(rows):
        shares[rows] = dot_last(gpre[rows], w_in[...])

    chunks(4, nrow, share)
    back_out[1] = shares[by_x_mate].astype(BF16)
    send(back_out.at[1], back_in.at[1], k_back + 1, mate)
    back_out[0] = shares[by_mate].astype(BF16)
    send(back_out.at[0], back_in.at[0], k_back, mate)
    arrive(back_in.at[1], k_back + 1)
    back_out[2] = (shares[by_x] + back_in[1].astype(F32)).astype(BF16)
    send(back_out.at[2], back_in.at[2], k_back + 2, across)
    for m, h in pieces_of:
        chain_step(1, m, h)
    sums[...] = jnp.zeros_like(sums)

    @pl.when(core == 1)
    def _():
        arrive(fin_in.at[3], k_fin_mate)

    arrive(fin_in.at[2], k_fin_anti)
    mine = fin_in[3].astype(F32) + fin_in[2].astype(F32)
    for c in range(2):
        for h in range(CUTS):
            arrive(fin_in.at[c, rows_of(h)], k_fin + c * CUTS + h)
        mine = mine + fin_in[c].astype(F32)

    prow = feat // npiece
    for p in range(npiece):
        pieces[p] = mine[p * prow : (p + 1) * prow].astype(BF16)
    for j, peer, p in scatter_peers:
        send(pieces.at[p], piece_in.at[j], k_piece + j, peer)

    arrive(back_in.at[0], k_back)
    arrive(back_in.at[2], k_back + 2)
    g_agg[...] = (shares[own] + back_in[0].astype(F32) + back_in[2].astype(F32)).astype(BF16)
    live_count = count_ref[0]

    def add_tile(t, carry):
        term = dot(tiles[t].T, g_agg[...])
        for k in range(3):
            on = jnp.logical_and(cols_ref[0, t] == k, t < live_count)
            sums[k] += term * jnp.where(on, 1.0, 0.0).astype(F32)
        return carry

    lax.fori_loop(0, tiles.shape[0], add_tile, 0)
    halo_out[0] = sums[0].astype(BF16)
    halo_out[1] = sums[2].astype(BF16)
    send(halo_out.at[0], halo_in.at[0], k_halo, prv)
    send(halo_out.at[1], halo_in.at[1], k_halo + 1, nxt)

    tot = pieces[my_piece].astype(F32)
    for j, peer, _ in scatter_peers:
        arrive(piece_in.at[j], k_piece + j)
        tot = tot + piece_in[j].astype(F32)
    triple[...] = tot.astype(BF16)
    for j, peer in tri_peers:
        send(triple, triple_in.at[zg], k_tri + j, peer)
    triple_in[zg] = triple[...]

    arrive(halo_in.at[0], k_halo)
    arrive(halo_in.at[1], k_halo + 1)
    centre = sums[1] + rows_c[own].astype(F32)
    nodes_buf[...] = (centre + halo_in[1].astype(F32) + halo_in[0].astype(F32)).astype(BF16)
    out_nodes = pltpu.make_async_copy(nodes_buf, nodes_ref, l_sem.at[0])
    out_nodes.start()

    for j, peer in tri_peers:
        arrive(triple_in.at[lax.rem(zg + zg_n - j, zg_n)], k_tri + j)
    tot = triple_in[0].astype(F32)
    for k in range(1, zg_n):
        tot = tot + triple_in[k].astype(F32)
    total[core, my_piece] = tot.astype(BF16)
    for j, peer, _ in scatter_peers:
        send(total.at[core, my_piece], total.at[core, my_piece], k_tot + j, peer)
    for j, peer, _ in scatter_peers:
        fxh = lax.rem(xh + X_HI - j // Z_IN, X_HI)
        fzi = lax.rem(zi + Z_IN - j % Z_IN, Z_IN)
        arrive(total.at[core, fxh * Z_IN + fzi], k_tot + j)
    send(total.at[core], total.at[core], k_swap, mate)
    arrive(total.at[other], k_swap)
    for p in range(npiece):
        gin_buf[p * prow : (p + 1) * prow, :] = total[0, p].astype(F32) * norm_factor
    out_gin = pltpu.make_async_copy(gin_buf, gin_ref, l_sem.at[1])
    out_gin.start()
    gout_buf[...] = jnp.concatenate([total[1, p] for p in range(npiece)], axis=0).T.astype(F32) * norm_factor
    out_gout = pltpu.make_async_copy(gout_buf, gout_ref, l_sem.at[2])
    out_gout.start()
    for copy in started:
        copy.wait_send()
    for only in range(2):

        @pl.when(core == only)
        def _():
            for make in started_on[only]:
                make().wait_send()

    out_nodes.wait()
    out_gin.wait()
    out_gout.wait()


def hand_over(*refs):
    n = len(refs) // 3
    sems = refs[-1]
    fetch = [pltpu.make_async_copy(refs[k], refs[2 * n + k], sems.at[k]) for k in range(n)]
    store = [pltpu.make_async_copy(refs[2 * n + k], refs[n + k], sems.at[n + k]) for k in range(n)]
    for copy in fetch:
        copy.start()
    for k in range(n):
        fetch[k].wait()
        store[k].start()
    for copy in store:
        copy.wait()


def local(nz, aggregated, cotangent, kernel_in, kernel_out, tile_values, tile_cols, tile_count):
    nrow, feat = aggregated.shape
    assert lax.axis_size("rep") == NY * X_LO
    hid = kernel_in.shape[1]
    slots = tile_values.shape[1]
    npiece = X_HI * Z_IN
    zg_n = nz // Z_IN
    prow = feat // npiece
    norm_factor = 1.0 / math.sqrt(nrow * lax.axis_size("node") * lax.axis_size("rep"))
    vmem = lambda shape, dtype=BF16: pltpu.VMEM(shape, dtype)
    hbm = pl.BlockSpec(memory_space=pltpu.HBM)
    scalars = pl.BlockSpec(memory_space=pltpu.SMEM)
    shapes = (
        jax.ShapeDtypeStruct((nrow, feat), BF16),
        jax.ShapeDtypeStruct((feat, hid), F32),
        jax.ShapeDtypeStruct((hid, feat), F32),
    )
    results = pl.pallas_call(
        functools.partial(kernel, nz, norm_factor),
        out_shape=shapes,
        in_specs=[hbm] * 5 + [scalars] * 2,
        out_specs=(hbm, hbm, hbm),
        scratch_shapes=[
            vmem((4 * nrow, feat)),
            vmem((4 * nrow, feat)),
            vmem((feat, 4 * nrow)),
            vmem((feat, 4 * nrow)),
            vmem((slots, nrow, nrow)),
            vmem((feat, HALF * hid)),
            vmem((HALF * hid, feat)),
            vmem((4 * nrow, HALF * hid)),
            vmem((4 * nrow, HALF * hid)),
            vmem((HALF, 2, feat, hid), F32),
            vmem((HALF, 2, feat, hid)),
            vmem((HALF, 2, feat, hid)),
            vmem((2, feat, hid)),
            vmem((4, feat, hid)),
            vmem((4 * nrow, feat), F32),
            vmem((3, nrow, feat), F32),
            vmem((nrow, feat)),
            vmem((3, nrow, feat)),
            vmem((3, nrow, feat)),
            vmem((2, nrow, feat)),
            vmem((2, nrow, feat)),
            vmem((npiece, prow, hid)),
            vmem((npiece, prow, hid)),
            vmem((prow, hid)),
            vmem((zg_n, prow, hid)),
            vmem((2, npiece, prow, hid)),
            vmem((nrow, feat)),
            vmem((feat, hid), F32),
            vmem((hid, feat), F32),
            pltpu.SemaphoreType.DMA((N_SEM,)),
            pltpu.SemaphoreType.DMA((N_SEM,)),
            pltpu.SemaphoreType.DMA((5,)),
        ],
        compiler_params=pltpu.CompilerParams(
            collective_id=0, has_side_effects=True, vmem_limit_bytes=62 << 20
        ),
    )(aggregated, cotangent, kernel_in, kernel_out, tile_values, tile_cols, tile_count)
    return pl.pallas_call(
        hand_over,
        out_shape=shapes,
        in_specs=[hbm] * 3,
        out_specs=(hbm, hbm, hbm),
        scratch_shapes=[vmem(s.shape, s.dtype) for s in shapes] + [pltpu.SemaphoreType.DMA((6,))],
        compiler_params=pltpu.CompilerParams(vmem_limit_bytes=62 << 20),
    )(*results)


def solution(mesh):
    nz = mesh.shape["node"] // (X_HI * CORES)
    return jax.shard_map(
        functools.partial(local, nz),
        mesh=mesh,
        in_specs=(
            P(("node", "rep"), None),
            P(("node", "rep"), None),
            P(None, "rep"),
            P("rep", None),
            P(("node", "rep"), None, None, None),
            P(("node", "rep"), None),
            P(("node", "rep")),
        ),
        out_specs=(P(("node", "rep"), None), P(None, "rep"), P("rep", None)),
        check_vma=False,
    )
```

```python
import functools
import math

import jax
import jax.numpy as jnp
from jax import lax
from jax.experimental import pallas as pl
from jax.experimental.pallas import tpu as pltpu
from jax.sharding import PartitionSpec as P

MESH = pl.DeviceIdType.MESH
BF16 = jnp.bfloat16
F32 = jnp.float32
X_HI, X_LO, CORES, NY, Z_IN = 2, 2, 2, 8, 4
HALF = NY // 2
GELU_C = math.sqrt(2.0 / math.pi)
N_SEM = 96
CUTS = 2


def dot(left, right):
    return jnp.dot(left, right, preferred_element_type=F32)


def dot_last(left, right):
    return lax.dot_general(left, right, (((1,), (1,)), ((), ())), preferred_element_type=F32)


def gelu_pair(pre, g_act):
    sq = pre * pre
    th = jnp.tanh(GELU_C * (pre + 0.044715 * sq * pre))
    half = 0.5 * (1.0 + th)
    slope = half + 0.5 * pre * (1.0 - th * th) * GELU_C * (1.0 + 3.0 * 0.044715 * sq)
    return (pre * half).astype(BF16), (g_act * slope).astype(BF16)


def kernel(
    nz, norm_factor,
    agg_ref, cot_ref, kin_ref, kout_ref, tiles_ref, cols_ref, count_ref,
    nodes_ref, gin_ref, gout_ref,
    rows_a, rows_c, at, ct, tiles, w_in, w_out, act, gpre, part, chain_out, chain_in, anti_out, fin_in,
    acc, back_out, back_in, halo_out, halo_in, pieces, piece_in, triple, triple_in, total,
    nodes_buf, gin_buf, gout_buf,
    s_sem, r_sem, l_sem,
):
    zg_n = nz // Z_IN
    npiece = X_HI * Z_IN
    nrow, feat = agg_ref.shape
    hid = kin_ref.shape[1]
    node, rep = lax.axis_index("node"), lax.axis_index("rep")
    core = lax.rem(node, CORES)
    z = lax.rem(lax.div(node, CORES), nz)
    xh = lax.div(node, CORES * nz)
    y, xl = lax.div(rep, X_LO), lax.rem(rep, X_LO)
    zg, zi = lax.div(z, Z_IN), lax.rem(z, Z_IN)
    other = 1 - core
    sign = 1 - 2 * core
    nodes = X_HI * nz * CORES

    def dev(xh, xl, y, z, core):
        return (xh * (nz * CORES) + z * CORES + core, y * X_LO + xl)

    def along_y(step, on_core):
        return dev(xh, xl, lax.rem(y + step + NY, NY), z, on_core)

    mate = dev(xh, xl, y, z, other)
    across = dev(lax.rem(xh + core, X_HI), 1 - xl, y, z, core)
    y_fwd, y_bwd = along_y(sign, core), along_y(-sign, core)
    nxt = (lax.rem(node + 1, nodes), rep)
    prv = (lax.rem(node + nodes - 1, nodes), rep)
    my_piece = xh * Z_IN + zi
    scatter_peers = []
    for j in range(npiece - 1, 0, -1):
        pxh = lax.rem(xh + j // Z_IN, X_HI)
        pzi = lax.rem(zi + j % Z_IN, Z_IN)
        scatter_peers.append((j, dev(pxh, xl, y, zg * Z_IN + pzi, core), pxh * Z_IN + pzi))
    tri_peers = []
    for j in range(1, zg_n):
        tri_peers.append((j, dev(xh, xl, y, lax.rem(zg + j, zg_n) * Z_IN + zi, core)))

    barrier = pltpu.get_barrier_semaphore()
    peers = [y_fwd, y_bwd, across, mate, along_y(sign, other), along_y(-sign, other)]
    peers += [along_y(HALF, core), along_y(HALF, other), nxt, prv]
    peers += [d for _, d, _ in scatter_peers] + [d for _, d in tri_peers]
    for peer in peers:
        pl.semaphore_signal(barrier, inc=1, device_id=peer, device_id_type=MESH)

    def in_slot(slot):
        start = slot * hid
        return pl.ds(start if isinstance(slot, int) else pl.multiple_of(start, hid), hid)

    own, by_mate, by_x, by_x_mate = [pl.ds(k * nrow, nrow) for k in range(4)]
    near, far = pl.ds(0, 2 * nrow), pl.ds(2 * nrow, 2 * nrow)
    every = pl.ds(0, 4 * nrow)
    loads = [
        pltpu.make_async_copy(agg_ref, rows_a.at[own], l_sem.at[0]),
        pltpu.make_async_copy(cot_ref, rows_c.at[own], l_sem.at[1]),
        pltpu.make_async_copy(tiles_ref.at[0], tiles, l_sem.at[2]),
    ]
    shard_loads = [
        pltpu.make_async_copy(kin_ref, w_in.at[:, in_slot(0)], l_sem.at[3]),
        pltpu.make_async_copy(kout_ref, w_out.at[in_slot(0)], l_sem.at[4]),
    ]
    for load in loads:
        load.start()

    @pl.when(core == 0)
    def _():
        for load in shard_loads:
            load.start()

    pl.semaphore_wait(barrier, len(peers))

    started = []
    started_on = ([], [])
    used = [0]

    def ids(count=1):
        used[0] += count
        return used[0] - count

    def copy_to(src, dst, k, device, k_recv=None):
        return pltpu.make_async_remote_copy(
            src_ref=src, dst_ref=dst, send_sem=s_sem.at[k], recv_sem=r_sem.at[k if k_recv is None else k_recv],
            device_id=device, device_id_type=MESH,
        )

    def send(src, dst, k, device, k_recv=None):
        copy = copy_to(src, dst, k, device, k_recv)
        copy.start()
        started.append(copy)

    def send_on(only, make):
        make().start()
        started_on[only].append(make)

    def settle():
        for copy in started:
            copy.wait_send()
        started.clear()
        for only in range(2):

            @pl.when(core == only)
            def _():
                for make in started_on[only]:
                    make().wait_send()

            started_on[only].clear()

    def arrive(dst, k):
        copy_to(dst, dst, k, mate).wait_recv()

    k_shard = [ids((HALF + 1) * CUTS) for _ in range(2)]
    k_mate_rows, k_x_rows, k_fwd_rows = ids(2), ids(2), ids(2)
    k_chain = ids(HALF * 2 * CUTS)
    k_fin, k_fin_anti, k_fin_mate = ids(4 * CUTS), ids(2), ids()
    k_back = ids(3)
    k_halo = ids(2)
    k_piece, k_tri, k_tot, k_swap = ids(npiece), ids(zg_n), ids(npiece), ids()
    assert used[0] <= N_SEM

    def w_at(m, slot, h):
        if m == 0:
            return w_in.at[pl.ds(h * (feat // CUTS), feat // CUTS), in_slot(slot)]
        size = hid // CUTS
        start = slot * hid + h * size
        return w_out.at[pl.ds(start if isinstance(slot, int) else pl.multiple_of(start, size), size)]

    pieces_of = [(m, h) for m in range(2) for h in range(CUTS)]

    def arrive_shard(m, h, j, slot):
        arrive(w_at(m, slot, h), k_shard[m] + j * CUTS + h)

    def forward_shard(m, h, j):
        send(w_at(m, j - core, h), w_at(m, j + 1 - core, h), k_shard[m] + (j + 1) * CUTS + h, y_fwd)

    for m, h in pieces_of:
        shard = (kin_ref, kout_ref)[m]
        size = shard.shape[0] // CUTS
        send(shard.at[pl.ds(h * size, size)], w_at(m, other, h), k_shard[m] + CUTS + h, y_fwd)
    send(agg_ref, rows_a.at[by_x], k_x_rows, across)
    send(cot_ref, rows_c.at[by_x], k_x_rows + 1, across)
    send(agg_ref, rows_a.at[by_mate], k_mate_rows, mate)
    send(cot_ref, rows_c.at[by_mate], k_mate_rows + 1, mate)

    def flip(block):
        at[:, block] = rows_a[block].T
        ct[:, block] = rows_c[block].T

    def unit(slot, rows):
        a, g = gelu_pair(dot(rows_a[rows], w_in[:, in_slot(slot)]), dot_last(rows_c[rows], w_out[in_slot(slot)]))
        act[rows, in_slot(slot)] = a
        gpre[rows, in_slot(slot)] = g

    def weight_term(slot, m):
        left, right = (at, gpre) if m == 0 else (ct, act)
        return dot(left[...], right[:, in_slot(slot)])

    for load in loads:
        load.wait()
    flip(own)
    arrive(rows_a.at[by_mate], k_mate_rows)
    arrive(rows_c.at[by_mate], k_mate_rows + 1)
    flip(by_mate)
    for m, h in pieces_of:
        arrive_shard(m, h, 1, 1 - core)
        forward_shard(m, h, 1)
    unit(1 - core, near)
    arrive(rows_a.at[by_x], k_x_rows)
    send(rows_a.at[by_x], rows_a.at[by_x_mate], k_fwd_rows, mate)
    for m, h in pieces_of:
        arrive_shard(m, h, 2, 2 - core)
        forward_shard(m, h, 2)
    arrive(rows_c.at[by_x], k_x_rows + 1)
    send(rows_c.at[by_x], rows_c.at[by_x_mate], k_fwd_rows + 1, mate)
    unit(2 - core, near)
    flip(by_x)
    arrive(rows_a.at[by_x_mate], k_fwd_rows)
    arrive(rows_c.at[by_x_mate], k_fwd_rows + 1)
    flip(by_x_mate)
    for m, h in pieces_of:
        arrive_shard(m, h, 3, 3 - core)

        @pl.when(core == 1)
        def _():
            send_on(1, lambda m=m, h=h: copy_to(w_at(m, 2, h), w_at(m, 3, h), k_shard[m] + HALF * CUTS + h, y_fwd))

    def rows_of(h):
        return pl.ds(h * (feat // CUTS), feat // CUTS)

    def k_link(k, m, h):
        return k_chain + (k * 2 + m) * CUTS + h

    unit(3 - core, every)
    for m in range(2):
        chain_out[3, m] = weight_term(3 - core, m).astype(BF16)
        for h in range(CUTS):
            send(chain_out.at[3, m, rows_of(h)], chain_in.at[3, m, rows_of(h)], k_link(3, m, h), y_bwd)
    for j in (2, 1):
        unit(j - core, far)
        for m in range(2):
            part[j, m] = weight_term(j - core, m)

    @pl.when(core == 0)
    def _():
        for load in shard_loads:
            load.wait()

    @pl.when(core == 1)
    def _():
        for m, h in pieces_of:
            arrive_shard(m, h, HALF, 3)

    unit(3 * core, every)
    for m in range(2):
        anti_out[m] = weight_term(3 * core, m).astype(BF16)

    @pl.when(core == 0)
    def _():
        send_on(0, lambda: copy_to(anti_out.at[1], fin_in.at[3], k_fin_mate, mate))
        fin_in[3] = anti_out[0]

    def shares(block):
        return dot_last(gpre[block], w_in[...])

    def chain_step(k, m, h):
        cut = rows_of(h)
        arrive(chain_in.at[k + 1, m, cut], k_link(k + 1, m, h))
        chain_out[k, m, cut] = (part[k, m, cut] + chain_in[k + 1, m, cut].astype(F32)).astype(BF16)
        if k > 1:
            send(chain_out.at[k, m, cut], chain_in.at[k, m, cut], k_link(k, m, h), y_bwd)
        else:
            to = along_y(-sign, m)
            send(chain_out.at[k, m, cut], fin_in.at[core, cut], k_fin + (2 + m) * CUTS + h, to, k_fin + core * CUTS + h)

    for m, h in pieces_of:
        chain_step(2, m, h)

    @pl.when(core == 1)
    def _():
        for m in range(2):
            send_on(1, lambda m=m: copy_to(anti_out.at[m], fin_in.at[2], k_fin_anti + m, along_y(HALF, m), k_fin_anti))

    back_out[1] = shares(by_x_mate).astype(BF16)
    send(back_out.at[1], back_in.at[1], k_back + 1, mate)
    back_out[0] = shares(by_mate).astype(BF16)
    send(back_out.at[0], back_in.at[0], k_back, mate)
    acc[...] = shares(by_x)
    arrive(back_in.at[1], k_back + 1)
    back_out[2] = (acc[...] + back_in[1].astype(F32)).astype(BF16)
    send(back_out.at[2], back_in.at[2], k_back + 2, across)
    for m, h in pieces_of:
        chain_step(1, m, h)
    acc[...] = shares(own)
    for t in range(tiles.shape[0]):
        tiles[t] = tiles[t].T

    @pl.when(core == 1)
    def _():
        arrive(fin_in.at[3], k_fin_mate)

    arrive(fin_in.at[2], k_fin_anti)
    mine = fin_in[3].astype(F32) + fin_in[2].astype(F32)
    for c in range(2):
        for h in range(CUTS):
            arrive(fin_in.at[c, rows_of(h)], k_fin + c * CUTS + h)
        mine = mine + fin_in[c].astype(F32)

    prow = feat // npiece
    for p in range(npiece):
        pieces[p] = mine[p * prow : (p + 1) * prow].astype(BF16)
    for j, peer, p in scatter_peers:
        send(pieces.at[p], piece_in.at[j], k_piece + j, peer)

    arrive(back_in.at[0], k_back)
    arrive(back_in.at[2], k_back + 2)
    g_agg = (acc[...] + back_in[0].astype(F32) + back_in[2].astype(F32)).astype(BF16)
    live_count = count_ref[0]
    sums = [None, None, None]
    for t in range(tiles.shape[0]):
        term = dot(tiles[t], g_agg)
        for k in range(3):
            on = jnp.logical_and(cols_ref[0, t] == k, t < live_count)
            add = term * jnp.where(on, 1.0, 0.0).astype(F32)
            sums[k] = add if sums[k] is None else sums[k] + add
    halo_out[0] = sums[0].astype(BF16)
    halo_out[1] = sums[2].astype(BF16)
    acc[...] = sums[1] + rows_c[own].astype(F32)
    settle()
    send(halo_out.at[0], halo_in.at[0], k_halo, prv)
    send(halo_out.at[1], halo_in.at[1], k_halo + 1, nxt)

    tot = pieces[my_piece].astype(F32)
    for j, peer, _ in scatter_peers:
        arrive(piece_in.at[j], k_piece + j)
        tot = tot + piece_in[j].astype(F32)
    triple[...] = tot.astype(BF16)
    for j, peer in tri_peers:
        send(triple, triple_in.at[zg], k_tri + j, peer)
    triple_in[zg] = triple[...]

    arrive(halo_in.at[0], k_halo)
    arrive(halo_in.at[1], k_halo + 1)
    nodes_buf[...] = (acc[...] + halo_in[1].astype(F32) + halo_in[0].astype(F32)).astype(BF16)
    out_nodes = pltpu.make_async_copy(nodes_buf, nodes_ref, l_sem.at[0])
    out_nodes.start()

    for j, peer in tri_peers:
        arrive(triple_in.at[lax.rem(zg + zg_n - j, zg_n)], k_tri + j)
    tot = triple_in[0].astype(F32)
    for k in range(1, zg_n):
        tot = tot + triple_in[k].astype(F32)
    total[core, my_piece] = tot.astype(BF16)
    for j, peer, _ in scatter_peers:
        send(total.at[core, my_piece], total.at[core, my_piece], k_tot + j, peer)
    for j, peer, _ in scatter_peers:
        fxh = lax.rem(xh + X_HI - j // Z_IN, X_HI)
        fzi = lax.rem(zi + Z_IN - j % Z_IN, Z_IN)
        arrive(total.at[core, fxh * Z_IN + fzi], k_tot + j)
    send(total.at[core], total.at[core], k_swap, mate)
    arrive(total.at[other], k_swap)
    for p in range(npiece):
        gin_buf[p * prow : (p + 1) * prow, :] = total[0, p].astype(F32) * norm_factor
    out_gin = pltpu.make_async_copy(gin_buf, gin_ref, l_sem.at[1])
    out_gin.start()
    gout_buf[...] = jnp.concatenate([total[1, p] for p in range(npiece)], axis=0).T.astype(F32) * norm_factor
    out_gout = pltpu.make_async_copy(gout_buf, gout_ref, l_sem.at[2])
    out_gout.start()
    for copy in started:
        copy.wait_send()
    out_nodes.wait()
    out_gin.wait()
    out_gout.wait()


def hand_over(*refs):
    n = len(refs) // 3
    sems = refs[-1]
    fetch = [pltpu.make_async_copy(refs[k], refs[2 * n + k], sems.at[k]) for k in range(n)]
    store = [pltpu.make_async_copy(refs[2 * n + k], refs[n + k], sems.at[n + k]) for k in range(n)]
    for copy in fetch:
        copy.start()
    for k in range(n):
        fetch[k].wait()
        store[k].start()
    for copy in store:
        copy.wait()


def local(nz, aggregated, cotangent, kernel_in, kernel_out, tile_values, tile_cols, tile_count):
    nrow, feat = aggregated.shape
    assert lax.axis_size("rep") == NY * X_LO
    hid = kernel_in.shape[1]
    slots = tile_values.shape[1]
    npiece = X_HI * Z_IN
    zg_n = nz // Z_IN
    prow = feat // npiece
    norm_factor = 1.0 / math.sqrt(nrow * lax.axis_size("node") * lax.axis_size("rep"))
    vmem = lambda shape, dtype=BF16: pltpu.VMEM(shape, dtype)
    hbm = pl.BlockSpec(memory_space=pltpu.HBM)
    scalars = pl.BlockSpec(memory_space=pltpu.SMEM)
    shapes = (
        jax.ShapeDtypeStruct((nrow, feat), BF16),
        jax.ShapeDtypeStruct((feat, hid), F32),
        jax.ShapeDtypeStruct((hid, feat), F32),
    )
    results = pl.pallas_call(
        functools.partial(kernel, nz, norm_factor),
        out_shape=shapes,
        in_specs=[hbm] * 5 + [scalars] * 2,
        out_specs=(hbm, hbm, hbm),
        scratch_shapes=[
            vmem((4 * nrow, feat)),
            vmem((4 * nrow, feat)),
            vmem((feat, 4 * nrow)),
            vmem((feat, 4 * nrow)),
            vmem((slots, nrow, nrow)),
            vmem((feat, HALF * hid)),
            vmem((HALF * hid, feat)),
            vmem((4 * nrow, HALF * hid)),
            vmem((4 * nrow, HALF * hid)),
            vmem((HALF, 2, feat, hid), F32),
            vmem((HALF, 2, feat, hid)),
            vmem((HALF, 2, feat, hid)),
            vmem((2, feat, hid)),
            vmem((4, feat, hid)),
            vmem((nrow, feat), F32),
            vmem((3, nrow, feat)),
            vmem((3, nrow, feat)),
            vmem((2, nrow, feat)),
            vmem((2, nrow, feat)),
            vmem((npiece, prow, hid)),
            vmem((npiece, prow, hid)),
            vmem((prow, hid)),
            vmem((zg_n, prow, hid)),
            vmem((2, npiece, prow, hid)),
            vmem((nrow, feat)),
            vmem((feat, hid), F32),
            vmem((hid, feat), F32),
            pltpu.SemaphoreType.DMA((N_SEM,)),
            pltpu.SemaphoreType.DMA((N_SEM,)),
            pltpu.SemaphoreType.DMA((5,)),
        ],
        compiler_params=pltpu.CompilerParams(
            collective_id=0, has_side_effects=True, vmem_limit_bytes=62 << 20
        ),
    )(aggregated, cotangent, kernel_in, kernel_out, tile_values, tile_cols, tile_count)
    return pl.pallas_call(
        hand_over,
        out_shape=shapes,
        in_specs=[hbm] * 3,
        out_specs=(hbm, hbm, hbm),
        scratch_shapes=[vmem(s.shape, s.dtype) for s in shapes] + [pltpu.SemaphoreType.DMA((6,))],
        compiler_params=pltpu.CompilerParams(vmem_limit_bytes=62 << 20),
    )(*results)


def solution(mesh):
    nz = mesh.shape["node"] // (X_HI * CORES)
    return jax.shard_map(
        functools.partial(local, nz),
        mesh=mesh,
        in_specs=(
            P(("node", "rep"), None),
            P(("node", "rep"), None),
            P(None, "rep"),
            P("rep", None),
            P(("node", "rep"), None, None, None),
            P(("node", "rep"), None),
            P(("node", "rep")),
        ),
        out_specs=(P(("node", "rep"), None), P(None, "rep"), P("rep", None)),
        check_vma=False,
    )
```

```python
import functools
import math

import jax
import jax.numpy as jnp
from jax import lax
from jax.experimental import pallas as pl
from jax.experimental.pallas import tpu as pltpu
from jax.sharding import PartitionSpec as P

MESH = pl.DeviceIdType.MESH
BF16 = jnp.bfloat16
F32 = jnp.float32
X_HI, X_LO, CORES, NY, Z_IN = 2, 2, 2, 8, 4
HALF = NY // 2
GELU_C = math.sqrt(2.0 / math.pi)
N_SEM = 96
CUTS = 2


def dot(left, right):
    return jnp.dot(left, right, preferred_element_type=F32)


def dot_last(left, right):
    return lax.dot_general(left, right, (((1,), (1,)), ((), ())), preferred_element_type=F32)


def gelu_pair(pre, g_act):
    sq = pre * pre
    th = jnp.tanh(GELU_C * (pre + 0.044715 * sq * pre))
    half = 0.5 * (1.0 + th)
    slope = half + 0.5 * pre * (1.0 - th * th) * GELU_C * (1.0 + 3.0 * 0.044715 * sq)
    return (pre * half).astype(BF16), (g_act * slope).astype(BF16)


def kernel(
    nz, norm_factor,
    agg_ref, cot_ref, kin_ref, kout_ref, tiles_ref, cols_ref, count_ref,
    nodes_ref, gin_ref, gout_ref,
    rows_a, rows_c, at, ct, tiles, w_in, w_out, act, gpre, part, chain_out, chain_in, anti_out, fin_in,
    acc, back_out, back_in, halo_out, halo_in, pieces, piece_in, triple, triple_in, total,
    s_sem, r_sem, l_sem,
):
    zg_n = nz // Z_IN
    npiece = X_HI * Z_IN
    nrow, feat = agg_ref.shape
    hid = kin_ref.shape[1]
    node, rep = lax.axis_index("node"), lax.axis_index("rep")
    core = lax.rem(node, CORES)
    z = lax.rem(lax.div(node, CORES), nz)
    xh = lax.div(node, CORES * nz)
    y, xl = lax.div(rep, X_LO), lax.rem(rep, X_LO)
    zg, zi = lax.div(z, Z_IN), lax.rem(z, Z_IN)
    other = 1 - core
    sign = 1 - 2 * core
    nodes = X_HI * nz * CORES

    def dev(xh, xl, y, z, core):
        return (xh * (nz * CORES) + z * CORES + core, y * X_LO + xl)

    def along_y(step, on_core):
        return dev(xh, xl, lax.rem(y + step + NY, NY), z, on_core)

    mate = dev(xh, xl, y, z, other)
    across = dev(lax.rem(xh + core, X_HI), 1 - xl, y, z, core)
    y_fwd, y_bwd = along_y(sign, core), along_y(-sign, core)
    nxt = (lax.rem(node + 1, nodes), rep)
    prv = (lax.rem(node + nodes - 1, nodes), rep)
    my_piece = xh * Z_IN + zi
    scatter_peers = []
    for j in range(npiece - 1, 0, -1):
        pxh = lax.rem(xh + j // Z_IN, X_HI)
        pzi = lax.rem(zi + j % Z_IN, Z_IN)
        scatter_peers.append((j, dev(pxh, xl, y, zg * Z_IN + pzi, core), pxh * Z_IN + pzi))
    tri_peers = []
    for j in range(1, zg_n):
        tri_peers.append((j, dev(xh, xl, y, lax.rem(zg + j, zg_n) * Z_IN + zi, core)))

    barrier = pltpu.get_barrier_semaphore()
    peers = [y_fwd, y_bwd, across, mate, along_y(sign, other), along_y(-sign, other)]
    peers += [nxt, prv]
    peers += [d for _, d, _ in scatter_peers] + [d for _, d in tri_peers]
    for peer in peers:
        pl.semaphore_signal(barrier, inc=1, device_id=peer, device_id_type=MESH)

    def in_slot(slot):
        start = slot * hid
        return pl.ds(start if isinstance(slot, int) else pl.multiple_of(start, hid), hid)

    own, by_mate, by_x, by_x_mate = [pl.ds(k * nrow, nrow) for k in range(4)]
    near, far = pl.ds(0, 2 * nrow), pl.ds(2 * nrow, 2 * nrow)
    every = pl.ds(0, 4 * nrow)
    loads = [
        pltpu.make_async_copy(agg_ref, rows_a.at[own], l_sem.at[0]),
        pltpu.make_async_copy(cot_ref, rows_c.at[own], l_sem.at[1]),
        pltpu.make_async_copy(tiles_ref.at[0], tiles, l_sem.at[2]),
    ]
    shard_loads = [
        pltpu.make_async_copy(kin_ref, w_in.at[:, in_slot(0)], l_sem.at[3]),
        pltpu.make_async_copy(kout_ref, w_out.at[in_slot(0)], l_sem.at[4]),
    ]
    for load in loads:
        load.start()

    @pl.when(core == 0)
    def _():
        for load in shard_loads:
            load.start()

    pl.semaphore_wait(barrier, len(peers))

    started = []
    started_on = ([], [])
    used = [0]

    def ids(count=1):
        used[0] += count
        return used[0] - count

    def copy_to(src, dst, k, device, k_recv=None):
        return pltpu.make_async_remote_copy(
            src_ref=src, dst_ref=dst, send_sem=s_sem.at[k], recv_sem=r_sem.at[k if k_recv is None else k_recv],
            device_id=device, device_id_type=MESH,
        )

    def send(src, dst, k, device, k_recv=None):
        copy = copy_to(src, dst, k, device, k_recv)
        copy.start()
        started.append(copy)

    def send_on(only, make):
        make().start()
        started_on[only].append(make)

    def settle():
        for copy in started:
            copy.wait_send()
        started.clear()
        for only in range(2):

            @pl.when(core == only)
            def _():
                for make in started_on[only]:
                    make().wait_send()

            started_on[only].clear()

    def arrive(dst, k):
        copy_to(dst, dst, k, mate).wait_recv()

    k_shard = [ids((HALF + 1) * CUTS) for _ in range(2)]
    k_mate_rows, k_x_rows, k_fwd_rows = ids(2), ids(2), ids(2)
    k_chain = ids(HALF * 2 * CUTS)
    k_fin, k_fin_anti, k_fin_mate = ids(4 * CUTS), ids(2), ids()
    k_back = ids(3)
    k_halo = ids(2)
    k_piece, k_tri, k_tot, k_swap = ids(npiece), ids(zg_n), ids(npiece), ids()
    assert used[0] <= N_SEM

    def w_at(m, slot, h):
        if m == 0:
            return w_in.at[pl.ds(h * (feat // CUTS), feat // CUTS), in_slot(slot)]
        size = hid // CUTS
        start = slot * hid + h * size
        return w_out.at[pl.ds(start if isinstance(slot, int) else pl.multiple_of(start, size), size)]

    pieces_of = [(m, h) for m in range(2) for h in range(CUTS)]

    def arrive_shard(m, h, j, slot):
        arrive(w_at(m, slot, h), k_shard[m] + j * CUTS + h)

    def forward_shard(m, h, j):
        send(w_at(m, j - core, h), w_at(m, j + 1 - core, h), k_shard[m] + (j + 1) * CUTS + h, y_fwd)

    for m, h in pieces_of:
        shard = (kin_ref, kout_ref)[m]
        size = shard.shape[0] // CUTS
        send(shard.at[pl.ds(h * size, size)], w_at(m, other, h), k_shard[m] + CUTS + h, y_fwd)
    send(agg_ref, rows_a.at[by_x], k_x_rows, across)
    send(cot_ref, rows_c.at[by_x], k_x_rows + 1, across)
    send(agg_ref, rows_a.at[by_mate], k_mate_rows, mate)
    send(cot_ref, rows_c.at[by_mate], k_mate_rows + 1, mate)

    def flip(block):
        at[:, block] = rows_a[block].T
        ct[:, block] = rows_c[block].T

    def unit(slot, rows):
        a, g = gelu_pair(dot(rows_a[rows], w_in[:, in_slot(slot)]), dot_last(rows_c[rows], w_out[in_slot(slot)]))
        act[rows, in_slot(slot)] = a
        gpre[rows, in_slot(slot)] = g

    def weight_term(slot, m):
        left, right = (at, gpre) if m == 0 else (ct, act)
        return dot(left[...], right[:, in_slot(slot)])

    for load in loads:
        load.wait()
    flip(own)
    arrive(rows_a.at[by_mate], k_mate_rows)
    arrive(rows_c.at[by_mate], k_mate_rows + 1)
    flip(by_mate)
    for m, h in pieces_of:
        arrive_shard(m, h, 1, 1 - core)
        forward_shard(m, h, 1)
    unit(1 - core, near)
    arrive(rows_a.at[by_x], k_x_rows)
    send(rows_a.at[by_x], rows_a.at[by_x_mate], k_fwd_rows, mate)
    for m, h in pieces_of:
        arrive_shard(m, h, 2, 2 - core)
        forward_shard(m, h, 2)
    arrive(rows_c.at[by_x], k_x_rows + 1)
    send(rows_c.at[by_x], rows_c.at[by_x_mate], k_fwd_rows + 1, mate)
    unit(2 - core, near)
    flip(by_x)
    arrive(rows_a.at[by_x_mate], k_fwd_rows)
    arrive(rows_c.at[by_x_mate], k_fwd_rows + 1)
    flip(by_x_mate)
    for m, h in pieces_of:
        arrive_shard(m, h, 3, 3 - core)

        @pl.when(core == 1)
        def _():
            send_on(1, lambda m=m, h=h: copy_to(w_at(m, 2, h), w_at(m, 3, h), k_shard[m] + HALF * CUTS + h, y_fwd))

    def rows_of(h):
        return pl.ds(h * (feat // CUTS), feat // CUTS)

    def k_link(k, m, h):
        return k_chain + (k * 2 + m) * CUTS + h

    unit(3 - core, every)
    for m in range(2):
        chain_out[3, m] = weight_term(3 - core, m).astype(BF16)
        for h in range(CUTS):
            send(chain_out.at[3, m, rows_of(h)], chain_in.at[3, m, rows_of(h)], k_link(3, m, h), y_bwd)
    for j in (2, 1):
        unit(j - core, far)
        for m in range(2):
            part[j, m] = weight_term(j - core, m)

    @pl.when(core == 0)
    def _():
        for load in shard_loads:
            load.wait()

    @pl.when(core == 1)
    def _():
        for m, h in pieces_of:
            arrive_shard(m, h, HALF, 3)

    unit(3 * core, every)
    for m in range(2):
        anti_out[m] = weight_term(3 * core, m).astype(BF16)

    @pl.when(core == 0)
    def _():
        send_on(0, lambda: copy_to(anti_out.at[1], fin_in.at[3], k_fin_mate, mate))
        fin_in[3] = anti_out[0]

    def shares(block):
        return dot_last(gpre[block], w_in[...])

    def chain_step(k, m, h):
        cut = rows_of(h)
        arrive(chain_in.at[k + 1, m, cut], k_link(k + 1, m, h))
        chain_out[k, m, cut] = (part[k, m, cut] + chain_in[k + 1, m, cut].astype(F32)).astype(BF16)
        if k > 1:
            send(chain_out.at[k, m, cut], chain_in.at[k, m, cut], k_link(k, m, h), y_bwd)
        else:
            to = along_y(-sign, m)
            send(chain_out.at[k, m, cut], fin_in.at[core, cut], k_fin + (2 + m) * CUTS + h, to, k_fin + core * CUTS + h)

    for m, h in pieces_of:
        chain_step(2, m, h)

    @pl.when(core == 1)
    def _():
        for m in range(2):
            send_on(1, lambda m=m: copy_to(anti_out.at[m], fin_in.at[2], k_fin_anti + m, along_y(HALF, m), k_fin_anti))

    back_out[1] = shares(by_x_mate).astype(BF16)
    send(back_out.at[1], back_in.at[1], k_back + 1, mate)
    back_out[0] = shares(by_mate).astype(BF16)
    send(back_out.at[0], back_in.at[0], k_back, mate)
    acc[...] = shares(by_x)
    arrive(back_in.at[1], k_back + 1)
    back_out[2] = (acc[...] + back_in[1].astype(F32)).astype(BF16)
    send(back_out.at[2], back_in.at[2], k_back + 2, across)
    for m, h in pieces_of:
        chain_step(1, m, h)
    acc[...] = shares(own)
    for t in range(tiles.shape[0]):
        tiles[t] = tiles[t].T

    @pl.when(core == 1)
    def _():
        arrive(fin_in.at[3], k_fin_mate)

    arrive(fin_in.at[2], k_fin_anti)
    mine = fin_in[3].astype(F32) + fin_in[2].astype(F32)
    for c in range(2):
        for h in range(CUTS):
            arrive(fin_in.at[c, rows_of(h)], k_fin + c * CUTS + h)
        mine = mine + fin_in[c].astype(F32)

    prow = feat // npiece
    for p in range(npiece):
        pieces[p] = mine[p * prow : (p + 1) * prow].astype(BF16)
    for j, peer, p in scatter_peers:
        send(pieces.at[p], piece_in.at[j], k_piece + j, peer)

    arrive(back_in.at[0], k_back)
    arrive(back_in.at[2], k_back + 2)
    g_agg = (acc[...] + back_in[0].astype(F32) + back_in[2].astype(F32)).astype(BF16)
    live_count = count_ref[0]
    sums = [None, None, None]
    for t in range(tiles.shape[0]):
        term = dot(tiles[t], g_agg)
        for k in range(3):
            on = jnp.logical_and(cols_ref[0, t] == k, t < live_count)
            add = term * jnp.where(on, 1.0, 0.0).astype(F32)
            sums[k] = add if sums[k] is None else sums[k] + add
    halo_out[0] = sums[0].astype(BF16)
    halo_out[1] = sums[2].astype(BF16)
    acc[...] = sums[1] + rows_c[own].astype(F32)
    settle()
    send(halo_out.at[0], halo_in.at[0], k_halo, prv)
    send(halo_out.at[1], halo_in.at[1], k_halo + 1, nxt)

    tot = pieces[my_piece].astype(F32)
    for j, peer, _ in scatter_peers:
        arrive(piece_in.at[j], k_piece + j)
        tot = tot + piece_in[j].astype(F32)
    triple[...] = tot.astype(BF16)
    for j, peer in tri_peers:
        send(triple, triple_in.at[zg], k_tri + j, peer)
    triple_in[zg] = triple[...]

    arrive(halo_in.at[0], k_halo)
    arrive(halo_in.at[1], k_halo + 1)
    nodes_ref[...] = (acc[...] + halo_in[1].astype(F32) + halo_in[0].astype(F32)).astype(BF16)

    for j, peer in tri_peers:
        arrive(triple_in.at[lax.rem(zg + zg_n - j, zg_n)], k_tri + j)
    tot = triple_in[0].astype(F32)
    for k in range(1, zg_n):
        tot = tot + triple_in[k].astype(F32)
    total[core, my_piece] = tot.astype(BF16)
    for j, peer, _ in scatter_peers:
        send(total.at[core, my_piece], total.at[core, my_piece], k_tot + j, peer)
    for j, peer, _ in scatter_peers:
        fxh = lax.rem(xh + X_HI - j // Z_IN, X_HI)
        fzi = lax.rem(zi + Z_IN - j % Z_IN, Z_IN)
        arrive(total.at[core, fxh * Z_IN + fzi], k_tot + j)
    send(total.at[core], total.at[core], k_swap, mate)
    arrive(total.at[other], k_swap)
    for p in range(npiece):
        gin_ref[p * prow : (p + 1) * prow, :] = total[0, p].astype(F32) * norm_factor
    gout_ref[...] = jnp.concatenate([total[1, p] for p in range(npiece)], axis=0).T.astype(F32) * norm_factor
    for copy in started:
        copy.wait_send()


def hand_over(*refs):
    n = len(refs) // 2
    store = [pltpu.make_async_copy(refs[k], refs[n + k], refs[-1].at[k]) for k in range(n)]
    for copy in store:
        copy.start()
    for copy in store:
        copy.wait()


def local(nz, aggregated, cotangent, kernel_in, kernel_out, tile_values, tile_cols, tile_count):
    nrow, feat = aggregated.shape
    assert lax.axis_size("rep") == NY * X_LO
    hid = kernel_in.shape[1]
    slots = tile_values.shape[1]
    npiece = X_HI * Z_IN
    zg_n = nz // Z_IN
    prow = feat // npiece
    norm_factor = 1.0 / math.sqrt(nrow * lax.axis_size("node") * lax.axis_size("rep"))
    vmem = lambda shape, dtype=BF16: pltpu.VMEM(shape, dtype)
    hbm = pl.BlockSpec(memory_space=pltpu.HBM)
    scalars = pl.BlockSpec(memory_space=pltpu.SMEM)
    shapes = (
        jax.ShapeDtypeStruct((nrow, feat), BF16),
        jax.ShapeDtypeStruct((feat, hid), F32),
        jax.ShapeDtypeStruct((hid, feat), F32),
    )
    results = pl.pallas_call(
        functools.partial(kernel, nz, norm_factor),
        out_shape=tuple(pltpu.VMEM(s.shape, s.dtype) for s in shapes),
        in_specs=[hbm] * 5 + [scalars] * 2,
        out_specs=(pl.BlockSpec(memory_space=pltpu.VMEM),) * 3,
        scratch_shapes=[
            vmem((4 * nrow, feat)),
            vmem((4 * nrow, feat)),
            vmem((feat, 4 * nrow)),
            vmem((feat, 4 * nrow)),
            vmem((slots, nrow, nrow)),
            vmem((feat, HALF * hid)),
            vmem((HALF * hid, feat)),
            vmem((4 * nrow, HALF * hid)),
            vmem((4 * nrow, HALF * hid)),
            vmem((HALF, 2, feat, hid), F32),
            vmem((HALF, 2, feat, hid)),
            vmem((HALF, 2, feat, hid)),
            vmem((2, feat, hid)),
            vmem((4, feat, hid)),
            vmem((nrow, feat), F32),
            vmem((3, nrow, feat)),
            vmem((3, nrow, feat)),
            vmem((2, nrow, feat)),
            vmem((2, nrow, feat)),
            vmem((npiece, prow, hid)),
            vmem((npiece, prow, hid)),
            vmem((prow, hid)),
            vmem((zg_n, prow, hid)),
            vmem((2, npiece, prow, hid)),
            pltpu.SemaphoreType.DMA((N_SEM,)),
            pltpu.SemaphoreType.DMA((N_SEM,)),
            pltpu.SemaphoreType.DMA((5,)),
        ],
        compiler_params=pltpu.CompilerParams(
            collective_id=0, has_side_effects=True, vmem_limit_bytes=40 << 20
        ),
    )(
        *[pltpu.with_memory_space_constraint(a, pltpu.HBM) for a in (aggregated, cotangent, kernel_in, kernel_out, tile_values)],
        tile_cols, tile_count,
    )
    return pl.pallas_call(
        hand_over,
        out_shape=shapes,
        in_specs=[pl.BlockSpec(memory_space=pltpu.VMEM)] * 3,
        out_specs=(hbm, hbm, hbm),
        scratch_shapes=[pltpu.SemaphoreType.DMA((3,))],
        compiler_params=pltpu.CompilerParams(vmem_limit_bytes=8 << 20),
    )(*results)


def solution(mesh):
    nz = mesh.shape["node"] // (X_HI * CORES)
    return jax.shard_map(
        functools.partial(local, nz),
        mesh=mesh,
        in_specs=(
            P(("node", "rep"), None),
            P(("node", "rep"), None),
            P(None, "rep"),
            P("rep", None),
            P(("node", "rep"), None, None, None),
            P(("node", "rep"), None),
            P(("node", "rep")),
        ),
        out_specs=(P(("node", "rep"), None), P(None, "rep"), P("rep", None)),
        check_vma=False,
    )
```
